128 devices in a mesh: pair: 8 (over y, z_lo), virt: 16 (over z_hi, x, core).
Axes of the slice: x: 4, y: 4, z: 4 (z_hi: 2, z_lo: 2; z = z_hi * 2 + z_lo), core: 2. Of those that a mesh axis runs over, the one named last changes fastest.
Arguments:
- amplitudes: float32 [4096, 16384], P('pair', 'virt'), may hold values from -6 to 6
- integrals: bfloat16 [16384, 16384], P('pair', 'virt'), may hold values from -0.046875 to 0.046875
- occ_energy: float32 [4096], P('pair'), may hold values from 0.5 to 4
- vir_energy: float32 [16384], P('virt'), may hold values from 0.5 to 4
- tile_mask: int32 [512, 128], P('pair', 'virt'), may hold values 0 or 1
- partner_slot: int32 [512, 128], P('pair', 'virt'), may hold values from 0 to 127, as said below
Outputs:
- new_amplitudes: float32 [4096, 16384], P('pair', 'virt')
The draws below stay inside these ranges and needn't reach their ends.
Inputs may be any that keep to these rules, and one draw needn't show every extreme that they name: `partner_slot`: within the block of tiles of each device (tile rows of one pair index by tile columns of one virt index), every device number 0 to 127 stands exactly 4 times, in an order drawn from the seed.
All inputs are finite; a program needn't handle non-finite values. No bound on the sum of `tile_mask` on one device may be relied on, other than what follows from the above.
Results may differ from the reference program's by a relative error of at most 0.0012.
Values may be sent and summed in bfloat16 or wider, within the bound.
No kernel may reach another device: no remote copies, remote signals or barrier semaphores. Data moves between devices by JAX's collectives and lax.ppermute only.
A program may use at most 128 MiB of HBM per device.

```python
import math
import jax
import jax.numpy as jnp
from jax import lax

VIR = 16384
TR = 8
TC = 128
OCC = 4096
COLS = 1024
NRT = 512
NCT = 128
RT_DEV = 64
CT_DEV = 8
TILES_DEV = 512
PER_PEER = 4
N_PAIR = 8
N_VIRT = 16
DEVICES = 128


def draw_partner_slot(key, part):
    base_slots = jnp.tile(jnp.arange(DEVICES, dtype=jnp.int32), PER_PEER)
    sub_keys = jax.random.split(key, DEVICES)

    def shuffled(sub_key):
        return base_slots[jax.random.permutation(sub_key, TILES_DEV)]
    device_slots = jax.vmap(shuffled)(sub_keys)
    arranged = device_slots.reshape(N_PAIR, N_VIRT, RT_DEV, CT_DEV).transpose(0, 2, 1, 3)
    return arranged.reshape(NRT, NCT).astype(jnp.int32)


def place_ends(drawn, stream_key, low, largest):
    dims = drawn.shape
    spot = [jax.random.randint(jax.random.fold_in(stream_key, axis), (), 0, dims[axis]) for axis in range(len(dims))]
    drawn = drawn.at[tuple(spot)].set(low)
    longest = dims.index(max(dims))
    spot[longest] = (spot[longest] + 1) % dims[longest]
    return drawn.at[tuple(spot)].set(largest)


def block_scale(own_key, shape, cuts, smallest, high):
    loudness = 1.0
    for dim, shards_of in cuts:
        heights = jax.random.uniform(jax.random.fold_in(jax.random.fold_in(own_key, 6), dim), (shards_of,), jnp.float32, smallest / len(cuts), high / len(cuts))
        loudness = loudness * jnp.repeat(jnp.exp(heights), shape[dim] // shards_of).reshape((-1,) + (1,) * (len(shape) - 1 - dim))
    return loudness


def gaussian(stream_key, shape, spread, reach, cuts=(), held_as=jnp.bfloat16):
    result = jax.random.normal(stream_key, shape, jnp.float32) * spread
    if len(cuts) > 0:
        result = block_scale(stream_key, shape, cuts, -0.22, 0.18) * result
    return jnp.clip(result, min=-reach, max=reach).astype(held_as)


def setup_inputs(seed: int = 0) -> dict:
    keys = jax.random.split(jax.random.key(seed), 7)
    return {
        "amplitudes": gaussian(keys[0], (OCC, VIR), 1.0, 6.0, ((0, 8), (1, 16)), jnp.float32),
        "integrals": gaussian(keys[1], (VIR, VIR), VIR ** -0.5, 0.046875, ((0, 8), (1, 16))),
        "occ_energy": jnp.clip(jnp.exp(math.log(4.0) - 2.0794415 * jax.random.uniform(keys[2], (OCC,), jnp.float32) ** block_scale(keys[2], (OCC,), ((0, 8),), -0.2, 0.2)), 0.5, 4.0),
        "vir_energy": jnp.clip(jnp.exp(math.log(4.0) - 2.0794415 * jax.random.uniform(keys[3], (VIR,), jnp.float32) ** block_scale(keys[3], (VIR,), ((0, 16),), -0.2, 0.2)), 0.5, 4.0),
        "tile_mask": place_ends((jax.random.randint(keys[4], (NRT, NCT), 0, 4) < 3).astype(jnp.int32), jax.random.fold_in(keys[4], 1), 0, 1),
        "partner_slot": draw_partner_slot(jax.random.fold_in(keys[6], 71), 0),
    }


def reference(amplitudes, integrals, occ_energy, vir_energy, tile_mask, partner_slot):
    amp_half = amplitudes.astype(jnp.bfloat16)
    blocks = integrals.reshape(VIR, N_VIRT, COLS).transpose(1, 0, 2)

    def column_block(block):
        return jnp.dot(amp_half, block, preferred_element_type=jnp.float32)

    product = lax.map(column_block, blocks)
    ladder = product.transpose(1, 0, 2).reshape(OCC, VIR)
    weights = tile_mask.astype(jnp.float32)
    masked = ladder.reshape(NRT, TR, NCT, TC) * weights[:, None, :, None]
    tiles = masked.reshape(N_PAIR, RT_DEV, TR, N_VIRT, CT_DEV, TC).transpose(0, 3, 1, 4, 2, 5).reshape(DEVICES, TILES_DEV, TR * TC)
    slots = partner_slot.reshape(N_PAIR, RT_DEV, N_VIRT, CT_DEV).transpose(0, 2, 1, 3).reshape(DEVICES, TILES_DEV)
    ordering = jnp.argsort(slots, axis=1, stable=True).astype(jnp.int32)
    inverse = jnp.argsort(ordering, axis=1, stable=True).astype(jnp.int32)
    outgoing = jnp.take_along_axis(tiles, ordering[:, :, None], axis=1).reshape(DEVICES, DEVICES, PER_PEER, TR * TC)
    incoming = outgoing.transpose(1, 0, 2, 3).reshape(DEVICES, TILES_DEV, TR * TC)
    partner = jnp.take_along_axis(incoming, inverse[:, :, None], axis=1)
    symmetric = (tiles + partner).reshape(N_PAIR, N_VIRT, RT_DEV, CT_DEV, TR, TC).transpose(0, 2, 4, 1, 3, 5).reshape(OCC, VIR)
    denominator = occ_energy[:, None] + vir_energy[None, :]
    return amplitudes - symmetric / denominator
```

```python
import functools
import jax
import jax.numpy as jnp
from jax import lax
from jax.experimental import pallas as pl
from jax.experimental.pallas import tpu as pltpu
from jax.sharding import PartitionSpec as P

TR = 8
TC = 128
AXES = ("pair", "virt")
BF = jnp.bfloat16
F32 = jnp.float32


def decode(device):
    p, v = divmod(device, 16)
    y, zl = divmod(p, 2)
    zh, r = divmod(v, 8)
    x, c = divmod(r, 2)
    return x, y, zl, zh, c


def encode(x, y, zl, zh, c):
    return ((y % 4) * 2 + zl % 2) * 16 + (zh % 2) * 8 + (x % 4) * 2 + c % 2


def permutation(move):
    return [(d, encode(*move(*decode(d)))) for d in range(128)]


def shift(dx=0, dy=0, dzl=0, dzh=0, dc=0):
    return permutation(lambda x, y, zl, zh, c: (x + dx, y + dy, zl + dzl, zh + dzh, c + dc))


def spread(a, b):
    def move(x, y, zl, zh, c):
        fy, fzl = 2 * zh + x // 2, x % 2
        return (y - fy + a, fy, fzl, zl ^ fzl, c ^ b)

    return permutation(move)


def send(value, pairs):
    return lax.ppermute(value, AXES, pairs)


VMEM = pl.BlockSpec(memory_space=pltpu.VMEM)
SMEM = pl.BlockSpec(memory_space=pltpu.SMEM)


def params(megabytes=56):
    return pltpu.CompilerParams(vmem_limit_bytes=megabytes << 20)


def cost(flops, moved):
    return pl.CostEstimate(flops=flops, bytes_accessed=moved, transcendentals=0)


def split_kernel(where, amp, *outs):
    for k, out in enumerate(outs):
        row = pl.multiple_of(where[k] * 64, 64)
        out[...] = amp[pl.ds(row, 64), :].astype(BF)


def split(amp, where):
    return pl.pallas_call(
        split_kernel,
        out_shape=[jax.ShapeDtypeStruct((64, 1024), BF)] * 8,
        in_specs=[SMEM, VMEM],
        out_specs=[VMEM] * 8,
        compiler_params=params(),
        cost_estimate=cost(0, 3 << 20),
        name="split",
    )(where, amp)


def join_kernel(where, *refs):
    out = refs[-1]
    for k in range(8):
        row = pl.multiple_of(where[2 * k] * 64, 64)
        col = pl.multiple_of(where[2 * k + 1] * 1024, 1024)
        out[pl.ds(row, 64), pl.ds(col, 1024)] = refs[k][...]


def join(pieces, where):
    return pl.pallas_call(
        join_kernel,
        out_shape=jax.ShapeDtypeStruct((256, 2048), BF),
        in_specs=[SMEM] + [VMEM] * 8,
        out_specs=VMEM,
        compiler_params=params(),
        cost_estimate=cost(0, 2 << 20),
        name="join",
    )(where, *pieces)


def product_kernel(counts, *refs):
    n_in = sum(counts)
    n = len(counts)
    blocks = refs[:n_in]
    own, oth = refs[n_in : n_in + 2]
    p0, p1, p2, p3 = refs[n_in + 2 : n_in + 6]
    held = refs[n_in + 6]
    step = pl.program_id(0)

    @pl.when(step == 0)
    def _():
        at = 0
        for ref in blocks:
            rows = ref.shape[0]
            held[at : at + rows, :] = ref[...]
            at += rows

    def run(b):
        r = jnp.dot(held[...], b[...], preferred_element_type=F32)
        for i in range(n):
            base = i * 256
            p0[i * 64 : i * 64 + 64, :] = r[base : base + 64]
            p1[i * 64 : i * 64 + 64, :] = r[base + 64 : base + 128].astype(BF)
            p2[i * 64 : i * 64 + 64, :] = r[base + 128 : base + 192].astype(BF)
            p3[i * 64 : i * 64 + 64, :] = r[base + 192 : base + 256].astype(BF)

    @pl.when(step < 2)
    def _():
        run(own)

    @pl.when(step >= 2)
    def _():
        run(oth)


def product(groups, own, oth):
    flat = [a for g in groups for a in g]
    counts = tuple(len(g) for g in groups)
    n = len(groups)
    whole = lambda a: pl.BlockSpec(a.shape, lambda s: (0, 0))
    return pl.pallas_call(
        functools.partial(product_kernel, counts),
        out_shape=[jax.ShapeDtypeStruct((n * 64, 2048), F32)]
        + [jax.ShapeDtypeStruct((n * 64, 2048), BF)] * 3,
        grid=(4,),
        in_specs=[whole(a) for a in flat]
        + [
            pl.BlockSpec((2048, 512), lambda s: (0, jnp.minimum(s, 1))),
            pl.BlockSpec((2048, 512), lambda s: (0, jnp.maximum(s - 2, 0))),
        ],
        out_specs=[pl.BlockSpec((n * 64, 512), lambda s: (0, s))] * 4,
        scratch_shapes=[pltpu.VMEM((n * 256, 2048), BF)],
        compiler_params=params(),
        cost_estimate=cost(2 * n * 256 * 2048 * 2048, (9 << 20) + n * (3 << 20)),
        name="product",
    )(*flat, own, oth)


def outgoing_kernel(place, mask, order, *refs):
    parts = refs[:8]
    masked, out = refs[8:]
    x = place[0]
    c = place[1]
    for i in range(4):
        for other in range(2):
            part = parts[other * 4 + i]
            chunk = lax.rem(x + i, 4) * 2 + (1 - c if other else c)
            for t in range(8):
                for k in range(8):
                    w = mask[(chunk * 8 + t) * 8 + k].astype(F32)
                    masked[pl.ds(pl.multiple_of(chunk * 64 + t * 8, 8), 8), k * 128 : k * 128 + 128] = (
                        part[t * 8 : t * 8 + 8, k * 128 : k * 128 + 128] * w
                    )

    def gather(s, carry):
        rows = []
        for j in range(4):
            t = order[s * 4 + j]
            row = pl.multiple_of(lax.shift_right_logical(t, 3) * 8, 8)
            col = pl.multiple_of(lax.bitwise_and(t, 7) * 128, 128)
            rows.append(masked[pl.ds(row, 8), pl.ds(col, 128)])
        out[s] = jnp.concatenate(rows, axis=0).astype(BF)
        return carry

    lax.fori_loop(0, 128, gather, 0, unroll=4)


def outgoing(place, mask, order, kept, swapped):
    return pl.pallas_call(
        outgoing_kernel,
        out_shape=[
            jax.ShapeDtypeStruct((512, 1024), F32),
            jax.ShapeDtypeStruct((128, 32, 128), BF),
        ],
        in_specs=[SMEM] * 3 + [VMEM] * 8,
        out_specs=[VMEM] * 2,
        compiler_params=params(),
        cost_estimate=cost(0, 5 << 20),
        name="outgoing",
    )(place, mask, order, *kept, *swapped)


def update_kernel(inverse, incoming, masked, amp, occ, vir, out, wide):
    wide[...] = incoming[...].astype(F32)

    def row(r, carry):
        at = pl.multiple_of(r * 8, 8)
        e = occ[pl.ds(at, 8), :]
        for k in range(8):
            q = inverse[r * 8 + k]
            partner = wide[pl.ds(pl.multiple_of(q * 8, 8), 8), :]
            cols = slice(k * 128, k * 128 + 128)
            symmetric = masked[pl.ds(at, 8), cols] + partner
            out[pl.ds(at, 8), cols] = amp[pl.ds(at, 8), cols] - symmetric / (e + vir[:, cols])
        return carry

    lax.fori_loop(0, 64, row, 0, unroll=2)


def update(inverse, incoming, masked, amp, occ, vir):
    return pl.pallas_call(
        update_kernel,
        out_shape=jax.ShapeDtypeStruct((512, 1024), F32),
        in_specs=[SMEM] + [VMEM] * 5,
        out_specs=VMEM,
        scratch_shapes=[pltpu.VMEM((4096, 128), F32)],
        compiler_params=params(),
        cost_estimate=cost(0, 7 << 20),
        name="update",
    )(inverse, incoming, masked, amp, occ, vir)


def shards(amplitudes, integrals, occ_energy, vir_energy, tile_mask, partner_slot):
    p, v = lax.axis_index("pair"), lax.axis_index("virt")
    y, zl = p // 2, p % 2
    zh, x, c = v // 8, (v // 2) % 4, v % 2
    fy = 2 * zh + x // 2

    where = jnp.stack([((y - fy + a) % 4) * 2 + (c ^ b) for a in range(4) for b in range(2)])
    pieces = split(amplitudes, where.astype(jnp.int32))
    moved = [send(pieces[2 * a + b], spread(a, b)) for a in range(4) for b in range(2)]
    where = jnp.stack([q for a in range(4) for b in range(2) for q in ((x - a) % 4, c ^ b)])
    own = integrals
    oth = send(integrals, shift(dc=1))
    block = {}
    block[0, 0] = join(moved, where.astype(jnp.int32))

    block[1, 0] = send(block[0, 0], shift(dx=-1))
    block[3, 0] = send(block[0, 0], shift(dx=1))
    block[0, 1] = send(block[0, 0], shift(dzh=1))
    block[1, 1] = send(block[0, 1], shift(dx=-1))
    block[3, 1] = send(block[0, 1], shift(dx=1))
    parts = {k: (b,) for k, b in block.items()}
    for j in range(2):
        parts[2, j] = (
            send(block[1, j][:128], shift(dx=-1)),
            send(block[3, j][128:], shift(dx=1)),
        )

    summed = {}
    for group in ([(0, 0)], [(0, 1), (1, 0), (3, 0)], [(1, 1), (3, 1)], [(2, 0), (2, 1)]):
        p0, p1, p2, p3 = product([parts[k] for k in group], own, oth)
        total = (
            p0
            + send(p1, shift(dy=1)).astype(F32)
            + send(p3, shift(dy=-1)).astype(F32)
            + send(p2, shift(dy=2)).astype(F32)
        )
        for n, k in enumerate(group):
            summed[k] = total[n * 64 : n * 64 + 64]

    kept, swapped = [None] * 4, [None] * 4
    low = zh == 0
    for group in ([0], [1, 3], [2]):
        stay = [jnp.where(low, summed[i, 0], summed[i, 1]) for i in group]
        leave = [jnp.where(low, summed[i, 1], summed[i, 0]).astype(BF) for i in group]
        got = send(jnp.concatenate(leave, axis=0), shift(dzl=1)).astype(F32)
        done = jnp.concatenate(stay, axis=0) + got
        crossed = send(done[:, 1024:], shift(dc=1))
        for n, i in enumerate(group):
            kept[i] = done[n * 64 : n * 64 + 64, :1024]
            swapped[i] = crossed[n * 64 : n * 64 + 64]

    slots = partner_slot.reshape(-1)
    order = jnp.argsort(slots, stable=True).astype(jnp.int32)
    inverse = jnp.argsort(order, stable=True).astype(jnp.int32)
    place = jnp.stack([x, c]).astype(jnp.int32)
    masked, out = outgoing(place, tile_mask.reshape(-1), order, kept, swapped)
    incoming = lax.all_to_all(out, AXES, split_axis=0, concat_axis=0, tiled=True)
    return update(
        inverse,
        incoming.reshape(4096, 128),
        masked,
        amplitudes,
        occ_energy[:, None],
        vir_energy[None, :],
    )


def solution(mesh):
    in_specs = (
        P("pair", "virt"),
        P("pair", "virt"),
        P("pair"),
        P("virt"),
        P("pair", "virt"),
        P("pair", "virt"),
    )
    out_specs = P("pair", "virt")
    return jax.shard_map(shards, mesh=mesh, in_specs=in_specs, out_specs=out_specs, check_vma=False)
```

```python
import functools
import jax
import jax.numpy as jnp
from jax import lax
from jax.experimental import pallas as pl
from jax.experimental.pallas import tpu as pltpu
from jax.sharding import PartitionSpec as P

AXES = ("pair", "virt")
BF = jnp.bfloat16
F32 = jnp.float32


def decode(device):
    p, v = divmod(device, 16)
    y, zl = divmod(p, 2)
    zh, r = divmod(v, 8)
    x, c = divmod(r, 2)
    return x, y, zl, zh, c


def encode(x, y, zl, zh, c):
    return ((y % 4) * 2 + zl % 2) * 16 + (zh % 2) * 8 + (x % 4) * 2 + c % 2


def permutation(move):
    return [(d, encode(*move(*decode(d)))) for d in range(128)]


def shift(dx=0, dy=0, dzl=0, dzh=0, dc=0):
    return permutation(lambda x, y, zl, zh, c: (x + dx, y + dy, zl + dzl, zh + dzh, c + dc))


def spread(a):
    def move(x, y, zl, zh, c):
        fy, fzl = 2 * zh + x // 2, x % 2
        return (y - fy + a, fy, fzl, zl ^ fzl, c)

    return permutation(move)


def send(value, pairs):
    return lax.ppermute(value, AXES, pairs)


VMEM = pl.BlockSpec(memory_space=pltpu.VMEM)
SMEM = pl.BlockSpec(memory_space=pltpu.SMEM)


def params(megabytes=56):
    return pltpu.CompilerParams(vmem_limit_bytes=megabytes << 20)


def cost(flops, moved):
    return pl.CostEstimate(flops=flops, bytes_accessed=moved, transcendentals=0)


def split_kernel(where, amp, keep, give):
    for k, out in enumerate((keep, give)):
        for a in range(4):
            row = pl.multiple_of(where[2 * a + k] * 64, 64)
            out[a * 64 : a * 64 + 64, :] = amp[pl.ds(row, 64), :].astype(BF)


def split(amp, where):
    return pl.pallas_call(
        split_kernel,
        out_shape=[jax.ShapeDtypeStruct((256, 1024), BF)] * 2,
        in_specs=[SMEM, VMEM],
        out_specs=[VMEM] * 2,
        compiler_params=params(),
        cost_estimate=cost(0, 3 << 20),
        name="split",
    )(where, amp)


def weave_kernel(where, keep, got, *outs):
    own = pl.multiple_of(where[0] * 1024, 1024)
    oth = pl.multiple_of(1024 - where[0] * 1024, 1024)
    for a, out in enumerate(outs):
        out[:, pl.ds(own, 1024)] = keep[a * 64 : a * 64 + 64, :]
        out[:, pl.ds(oth, 1024)] = got[a * 64 : a * 64 + 64, :]


def weave(where, keep, got):
    return pl.pallas_call(
        weave_kernel,
        out_shape=[jax.ShapeDtypeStruct((64, 2048), BF)] * 4,
        in_specs=[SMEM] + [VMEM] * 2,
        out_specs=[VMEM] * 4,
        compiler_params=params(),
        cost_estimate=cost(0, 2 << 20),
        name="weave",
    )(where, keep, got)


def join_kernel(where, *refs):
    out = refs[-1]
    for a in range(4):
        out[pl.ds(pl.multiple_of(where[a] * 64, 64), 64), :] = refs[a][...]


def join(where, pieces):
    return pl.pallas_call(
        join_kernel,
        out_shape=jax.ShapeDtypeStruct((256, 2048), BF),
        in_specs=[SMEM] + [VMEM] * 4,
        out_specs=VMEM,
        compiler_params=params(),
        cost_estimate=cost(0, 2 << 20),
        name="join",
    )(where, *pieces)


def product_kernel(counts, *refs):
    n_in = sum(counts)
    n = len(counts)
    blocks = refs[:n_in]
    own, oth = refs[n_in : n_in + 2]
    p0, p1, p2, p3 = refs[n_in + 2 : n_in + 6]
    held = refs[n_in + 6]
    step = pl.program_id(0)

    @pl.when(step == 0)
    def _():
        at = 0
        for ref in blocks:
            rows = ref.shape[0]
            held[at : at + rows, :] = ref[...]
            at += rows

    def run(b):
        r = jnp.dot(held[...], b[...], preferred_element_type=F32)
        for i in range(n):
            base = i * 256
            p0[i * 64 : i * 64 + 64, :] = r[base : base + 64]
            p1[i * 64 : i * 64 + 64, :] = r[base + 64 : base + 128].astype(BF)
            p2[i * 64 : i * 64 + 64, :] = r[base + 128 : base + 192].astype(BF)
            p3[i * 64 : i * 64 + 64, :] = r[base + 192 : base + 256].astype(BF)

    @pl.when(step < 2)
    def _():
        run(own)

    @pl.when(step >= 2)
    def _():
        run(oth)


def product(groups, own, oth):
    flat = [a for g in groups for a in g]
    counts = tuple(len(g) for g in groups)
    n = len(groups)
    whole = lambda a: pl.BlockSpec(a.shape, lambda s: (0, 0))
    return pl.pallas_call(
        functools.partial(product_kernel, counts),
        out_shape=[jax.ShapeDtypeStruct((n * 64, 2048), F32)]
        + [jax.ShapeDtypeStruct((n * 64, 2048), BF)] * 3,
        grid=(4,),
        in_specs=[whole(a) for a in flat]
        + [
            pl.BlockSpec((2048, 512), lambda s: (0, jnp.minimum(s, 1))),
            pl.BlockSpec((2048, 512), lambda s: (0, jnp.maximum(s - 2, 0))),
        ],
        out_specs=[pl.BlockSpec((n * 64, 512), lambda s: (0, s))] * 4,
        scratch_shapes=[pltpu.VMEM((n * 256, 2048), BF)],
        compiler_params=params(),
        cost_estimate=cost(2 * n * 256 * 2048 * 2048, (9 << 20) + n * (3 << 20)),
        name="product",
    )(*flat, own, oth)


def outgoing_kernel(place, mask, order, *refs):
    parts = refs[:8]
    masked, out = refs[8:]
    x = place[0]
    c = place[1]
    for i in range(4):
        for other in range(2):
            part = parts[other * 4 + i]
            chunk = lax.rem(x + i, 4) * 2 + (1 - c if other else c)
            for t in range(8):
                for k in range(8):
                    w = mask[(chunk * 8 + t) * 8 + k].astype(F32)
                    masked[pl.ds(pl.multiple_of(chunk * 64 + t * 8, 8), 8), k * 128 : k * 128 + 128] = (
                        part[t * 8 : t * 8 + 8, k * 128 : k * 128 + 128] * w
                    )

    def gather(s, carry):
        rows = []
        for j in range(4):
            t = order[s * 4 + j]
            row = pl.multiple_of(lax.shift_right_logical(t, 3) * 8, 8)
            col = pl.multiple_of(lax.bitwise_and(t, 7) * 128, 128)
            rows.append(masked[pl.ds(row, 8), pl.ds(col, 128)])
        out[s] = jnp.concatenate(rows, axis=0).astype(BF)
        return carry

    lax.fori_loop(0, 128, gather, 0, unroll=4)


def outgoing(place, mask, order, kept, swapped):
    return pl.pallas_call(
        outgoing_kernel,
        out_shape=[
            jax.ShapeDtypeStruct((512, 1024), F32),
            jax.ShapeDtypeStruct((128, 32, 128), BF),
        ],
        in_specs=[SMEM] * 3 + [VMEM] * 8,
        out_specs=[VMEM] * 2,
        compiler_params=params(),
        cost_estimate=cost(0, 5 << 20),
        name="outgoing",
    )(place, mask, order, *kept, *swapped)


def update_kernel(inverse, incoming, masked, amp, occ, vir, out, wide):
    wide[...] = incoming[...].astype(F32)

    def row(r, carry):
        at = pl.multiple_of(r * 8, 8)
        e = occ[pl.ds(at, 8), :]
        for k in range(8):
            q = inverse[r * 8 + k]
            partner = wide[pl.ds(pl.multiple_of(q * 8, 8), 8), :]
            cols = slice(k * 128, k * 128 + 128)
            symmetric = masked[pl.ds(at, 8), cols] + partner
            out[pl.ds(at, 8), cols] = amp[pl.ds(at, 8), cols] - symmetric / (e + vir[:, cols])
        return carry

    lax.fori_loop(0, 64, row, 0, unroll=2)


def update(inverse, incoming, masked, amp, occ, vir):
    return pl.pallas_call(
        update_kernel,
        out_shape=jax.ShapeDtypeStruct((512, 1024), F32),
        in_specs=[SMEM] + [VMEM] * 5,
        out_specs=VMEM,
        scratch_shapes=[pltpu.VMEM((4096, 128), F32)],
        compiler_params=params(),
        cost_estimate=cost(0, 7 << 20),
        name="update",
    )(inverse, incoming, masked, amp, occ, vir)


GROUPS = (((0, 0),), ((0, 1), (1, 0), (3, 0)), ((1, 1), (3, 1)), ((2, 0), (2, 1)))
LAST = ((0,), (1, 3), (2,))


def compute(amplitudes, integrals, occ_energy, vir_energy, tile_mask, partner_slot):
    device = lax.axis_index(AXES)
    c, x, zh = device & 1, (device >> 1) & 3, (device >> 3) & 1
    y = (device >> 5) & 3
    fy = 2 * zh + (x >> 1)

    where = jnp.stack([((y - fy + a) & 3) * 2 + (c ^ b) for a in range(4) for b in range(2)])
    keep, give = split(amplitudes, where)
    got = send(give, shift(dc=1))
    pieces = weave(c[None], keep, got)
    moved = [send(pieces[a], spread(a)) for a in range(4)]
    own = integrals
    oth = send(integrals, shift(dc=1))
    block = {}
    block[0, 0] = join(jnp.stack([(x - a) & 3 for a in range(4)]), moved)

    block[1, 0] = send(block[0, 0], shift(dx=-1))
    block[3, 0] = send(block[0, 0], shift(dx=1))
    block[0, 1] = send(block[0, 0], shift(dzh=1))
    block[1, 1] = send(block[0, 1], shift(dx=-1))
    block[3, 1] = send(block[0, 1], shift(dx=1))
    parts = {k: (b,) for k, b in block.items()}
    for j in range(2):
        parts[2, j] = (
            send(block[1, j][:128], shift(dx=-1)), send(block[3, j][128:], shift(dx=1))
        )

    summed = {}
    for group in GROUPS:
        p0, p1, p2, p3 = product([parts[k] for k in group], own, oth)
        q2 = send(p2, shift(dy=2))
        q1 = send(p1, shift(dy=1))
        q3 = send(p3, shift(dy=-1))
        total = p0 + q1.astype(F32) + q3.astype(F32) + q2.astype(F32)
        for n, k in enumerate(group):
            summed[k] = total[n * 64 : n * 64 + 64]

    kept, swapped = [None] * 4, [None] * 4
    low = zh == 0
    for group in LAST:
        stay = [jnp.where(low, summed[i, 0], summed[i, 1]) for i in group]
        leave = [jnp.where(low, summed[i, 1], summed[i, 0]).astype(BF) for i in group]
        got = send(jnp.concatenate(leave, axis=0), shift(dzl=1)).astype(F32)
        done = jnp.concatenate(stay, axis=0) + got
        crossed = send(done[:, 1024:], shift(dc=1))
        for n, i in enumerate(group):
            kept[i] = done[n * 64 : n * 64 + 64, :1024]
            swapped[i] = crossed[n * 64 : n * 64 + 64]

    slots = partner_slot.reshape(-1)
    order = jnp.argsort(slots, stable=True).astype(jnp.int32)
    inverse = jnp.argsort(order, stable=True).astype(jnp.int32)
    place = jnp.stack([x, c])
    masked, out = outgoing(place, tile_mask.reshape(-1), order, kept, swapped)
    incoming = lax.all_to_all(out, AXES, split_axis=0, concat_axis=0, tiled=True)
    return update(
        inverse,
        incoming.reshape(4096, 128),
        masked,
        amplitudes,
        occ_energy[:, None],
        vir_energy[None, :],
    )


def solution(mesh):
    in_specs = (
        P("pair", "virt"),
        P("pair", "virt"),
        P("pair"),
        P("virt"),
        P("pair", "virt"),
        P("pair", "virt"),
    )
    out_specs = P("pair", "virt")
    return jax.shard_map(compute, mesh=mesh, in_specs=in_specs, out_specs=out_specs, check_vma=False)
```

```python
import functools
import jax
import jax.numpy as jnp
from jax import lax
from jax.experimental import pallas as pl
from jax.experimental.pallas import tpu as pltpu
from jax.sharding import PartitionSpec as P

AXES = ("pair", "virt")
BF = jnp.bfloat16
F32 = jnp.float32


def decode(device):
    p, v = divmod(device, 16)
    y, zl = divmod(p, 2)
    zh, r = divmod(v, 8)
    x, c = divmod(r, 2)
    return x, y, zl, zh, c


def encode(x, y, zl, zh, c):
    return ((y % 4) * 2 + zl % 2) * 16 + (zh % 2) * 8 + (x % 4) * 2 + c % 2


def permutation(move):
    return [(d, encode(*move(*decode(d)))) for d in range(128)]


def shift(dx=0, dy=0, dzl=0, dzh=0, dc=0):
    return permutation(lambda x, y, zl, zh, c: (x + dx, y + dy, zl + dzl, zh + dzh, c + dc))


def spread(a):
    def move(x, y, zl, zh, c):
        fy, fzl = 2 * zh + x // 2, x % 2
        return (y - fy + a, y, fzl, zl ^ fzl, c)

    return permutation(move)


def settle(a):
    return permutation(lambda x, y, zl, zh, c: (x, y - x + a, zl, zh, c))


def send(value, pairs):
    return lax.ppermute(value, AXES, pairs)


VMEM = pl.BlockSpec(memory_space=pltpu.VMEM)
SMEM = pl.BlockSpec(memory_space=pltpu.SMEM)


def params(megabytes=56):
    return pltpu.CompilerParams(vmem_limit_bytes=megabytes << 20)


def cost(flops, moved):
    return pl.CostEstimate(flops=flops, bytes_accessed=moved, transcendentals=0)


def split_kernel(where, amp, keep, give):
    for k, out in enumerate((keep, give)):
        for a in range(4):
            row = pl.multiple_of(where[2 * a + k] * 64, 64)
            out[a * 64 : a * 64 + 64, :] = amp[pl.ds(row, 64), :].astype(BF)


def split(amp, where):
    return pl.pallas_call(
        split_kernel,
        out_shape=[jax.ShapeDtypeStruct((256, 1024), BF)] * 2,
        in_specs=[SMEM, VMEM],
        out_specs=[VMEM] * 2,
        compiler_params=params(),
        cost_estimate=cost(0, 3 << 20),
        name="split",
    )(where, amp)


def weave_kernel(where, keep, got, *outs):
    own = pl.multiple_of(where[0] * 1024, 1024)
    oth = pl.multiple_of(1024 - where[0] * 1024, 1024)
    for a, out in enumerate(outs):
        out[:, pl.ds(own, 1024)] = keep[a * 64 : a * 64 + 64, :]
        out[:, pl.ds(oth, 1024)] = got[a * 64 : a * 64 + 64, :]


def weave(where, keep, got):
    return pl.pallas_call(
        weave_kernel,
        out_shape=[jax.ShapeDtypeStruct((64, 2048), BF)] * 4,
        in_specs=[SMEM] + [VMEM] * 2,
        out_specs=[VMEM] * 4,
        compiler_params=params(),
        cost_estimate=cost(0, 2 << 20),
        name="weave",
    )(where, keep, got)


def join_kernel(where, *refs):
    out = refs[-1]
    for a in range(4):
        out[pl.ds(pl.multiple_of(where[a] * 64, 64), 64), :] = refs[a][...]


def join(where, pieces):
    return pl.pallas_call(
        join_kernel,
        out_shape=jax.ShapeDtypeStruct((256, 2048), BF),
        in_specs=[SMEM] + [VMEM] * 4,
        out_specs=VMEM,
        compiler_params=params(),
        cost_estimate=cost(0, 2 << 20),
        name="join",
    )(where, *pieces)


def product_kernel(counts, *refs):
    n_in = sum(counts)
    n = len(counts)
    blocks = refs[:n_in]
    own, oth = refs[n_in : n_in + 2]
    zero_a, zero_b, one_a, three_b, up, down = refs[n_in + 2 : n_in + 8]
    held = refs[n_in + 8]
    step = pl.program_id(0)

    @pl.when(step == 0)
    def _():
        at = 0
        for ref in blocks:
            rows = ref.shape[0]
            held[at : at + rows, :] = ref[...]
            at += rows

    def rows_of(r, i, k):
        return r[i * 256 + k * 64 : i * 256 + k * 64 + 64]

    @pl.when(step < 2)
    def _():
        r = jnp.dot(held[...], own[...], preferred_element_type=F32)
        for i in range(n):
            at = slice(i * 64, i * 64 + 64)
            zero_a[at, :] = rows_of(r, i, 0)
            one_a[at, :] = rows_of(r, i, 1)
            up[at, :] = rows_of(r, i, 2).astype(BF)
            down[at, :] = rows_of(r, i, 3).astype(BF)

    @pl.when(step >= 2)
    def _():
        r = jnp.dot(held[...], oth[...], preferred_element_type=F32)
        for i in range(n):
            at = slice(i * 64, i * 64 + 64)
            zero_b[at, :] = rows_of(r, i, 0)
            up[at, :] = rows_of(r, i, 1).astype(BF)
            down[at, :] = rows_of(r, i, 2).astype(BF)
            three_b[at, :] = rows_of(r, i, 3)


def product(groups, own, oth):
    flat = [a for g in groups for a in g]
    counts = tuple(len(g) for g in groups)
    n = len(groups)
    whole = lambda a: pl.BlockSpec(a.shape, lambda s: (0, 0))
    first = lambda s: (0, jnp.minimum(s, 1))
    second = lambda s: (0, jnp.maximum(s - 2, 0))
    half = jax.ShapeDtypeStruct((n * 64, 1024), F32)
    full = jax.ShapeDtypeStruct((n * 64, 2048), BF)
    out = lambda at: pl.BlockSpec((n * 64, 512), at)
    return pl.pallas_call(
        functools.partial(product_kernel, counts),
        out_shape=[half] * 4 + [full] * 2,
        grid=(4,),
        in_specs=[whole(a) for a in flat]
        + [pl.BlockSpec((2048, 512), first), pl.BlockSpec((2048, 512), second)],
        out_specs=[out(first), out(second), out(first), out(second)]
        + [out(lambda s: (0, s))] * 2,
        scratch_shapes=[pltpu.VMEM((n * 256, 2048), BF)],
        compiler_params=params(),
        cost_estimate=cost(2 * n * 256 * 2048 * 2048, (9 << 20) + n * (3 << 20)),
        name="product",
    )(*flat, own, oth)


def settle_kernel(n_groups, members, low, *refs):
    ins, outs = refs[: 6 * n_groups], refs[6 * n_groups :]
    stay_a, stay_b, leave_a, leave_b = outs

    def total(g, n):
        za, zb, up, down, nup, ndown = ins[6 * g : 6 * g + 6]
        at = slice(n * 64, n * 64 + 64)
        a = za[at, :] + down[at, :1024].astype(F32) + nup[at, :].astype(F32)
        b = zb[at, :] + up[at, 1024:].astype(F32) + ndown[at, :].astype(F32)
        return a, b

    def write(swap):
        for k, (c0, c1) in enumerate(members):
            at = slice(k * 64, k * 64 + 64)
            a, b = total(*(c1 if swap else c0))
            stay_a[at, :] = a
            stay_b[at, :] = b
            a, b = total(*(c0 if swap else c1))
            leave_a[at, :] = a.astype(BF)
            leave_b[at, :] = b.astype(BF)

    @pl.when(low[0] == 1)
    def _():
        write(False)

    @pl.when(low[0] == 0)
    def _():
        write(True)


def collect(low, groups, members):
    rows = 64 * len(members)
    flat = [a for g in groups for a in g]
    return pl.pallas_call(
        functools.partial(settle_kernel, len(groups), members),
        out_shape=[jax.ShapeDtypeStruct((rows, 1024), F32)] * 2
        + [jax.ShapeDtypeStruct((rows, 1024), BF)] * 2,
        in_specs=[SMEM] + [VMEM] * len(flat),
        out_specs=[VMEM] * 4,
        compiler_params=params(),
        cost_estimate=cost(0, rows * 1024 * 24),
        name="collect",
    )(low, *flat)


def outgoing_kernel(code, *refs):
    full, out = refs[-2:]
    at = 0
    for k in (0, 2):
        for g in range(2):
            stay, got = refs[4 * g + k : 4 * g + k + 2]
            rows = stay.shape[0]
            full[at : at + rows, :] = stay[...] + got[...].astype(F32)
            at += rows

    def gather(s, carry):
        rows = []
        for j in range(4):
            q = code[s * 4 + j]
            row = pl.multiple_of(lax.shift_right_logical(q, 4) * 8, 8)
            col = pl.multiple_of(lax.bitwise_and(lax.shift_right_logical(q, 1), 7) * 128, 128)
            w = lax.bitwise_and(q, 1).astype(F32)
            rows.append(full[pl.ds(row, 8), pl.ds(col, 128)] * w)
        out[s] = jnp.concatenate(rows, axis=0).astype(BF)
        return carry

    lax.fori_loop(0, 128, gather, 0, unroll=4)


def outgoing(code, *parts):
    return pl.pallas_call(
        outgoing_kernel,
        out_shape=[
            jax.ShapeDtypeStruct((512, 1024), F32),
            jax.ShapeDtypeStruct((128, 32, 128), BF),
        ],
        in_specs=[SMEM] + [VMEM] * 8,
        out_specs=[VMEM] * 2,
        compiler_params=params(),
        cost_estimate=cost(0, 6 << 20),
        name="outgoing",
    )(code, *parts)


def base_kernel(row_of, mask, full, amp, occ, vir, base, scale):
    def row(r, carry):
        at = pl.multiple_of(r * 8, 8)
        src = pl.multiple_of(row_of[r], 8)
        e = occ[pl.ds(at, 8), :]
        for k in range(8):
            w = mask[r * 8 + k].astype(F32)
            cols = slice(k * 128, k * 128 + 128)
            q = 1.0 / (e + vir[:, cols])
            scale[pl.ds(at, 8), cols] = q
            base[pl.ds(at, 8), cols] = amp[pl.ds(at, 8), cols] - full[pl.ds(src, 8), cols] * w * q
        return carry

    lax.fori_loop(0, 64, row, 0, unroll=2)


def make_base(row_of, mask, full, amp, occ, vir):
    return pl.pallas_call(
        base_kernel,
        out_shape=[jax.ShapeDtypeStruct((512, 1024), F32)] * 2,
        in_specs=[SMEM] * 2 + [VMEM] * 4,
        out_specs=[VMEM] * 2,
        compiler_params=params(),
        cost_estimate=cost(0, 8 << 20),
        name="base",
    )(row_of, mask, full, amp, occ, vir)


def update_kernel(inverse, incoming, base, scale, out, wide):
    wide[...] = incoming[...].astype(F32)

    def row(r, carry):
        at = pl.multiple_of(r * 8, 8)
        for k in range(8):
            q = inverse[r * 8 + k]
            partner = wide[pl.ds(pl.multiple_of(q * 8, 8), 8), :]
            cols = slice(k * 128, k * 128 + 128)
            out[pl.ds(at, 8), cols] = base[pl.ds(at, 8), cols] - partner * scale[pl.ds(at, 8), cols]
        return carry

    lax.fori_loop(0, 64, row, 0, unroll=4)


def update(inverse, incoming, base, scale):
    return pl.pallas_call(
        update_kernel,
        out_shape=jax.ShapeDtypeStruct((512, 1024), F32),
        in_specs=[SMEM] + [VMEM] * 3,
        out_specs=VMEM,
        scratch_shapes=[pltpu.VMEM((4096, 128), F32)],
        compiler_params=params(),
        cost_estimate=cost(0, 7 << 20),
        name="update",
    )(inverse, incoming, base, scale)


GROUPS = (((0, 0),), ((0, 1), (1, 0), (3, 0)), ((1, 1), (3, 1)), ((2, 0), (2, 1)))
LAST = (
    ((0, 1, 2), (((0, 0), (1, 0)), ((1, 1), (2, 0)), ((1, 2), (2, 1)))),
    ((3,), (((0, 0), (0, 1)),)),
)


def compute(amplitudes, integrals, occ_energy, vir_energy, tile_mask, partner_slot):
    device = lax.axis_index(AXES)
    c, x, zh = device & 1, (device >> 1) & 3, (device >> 3) & 1
    y = (device >> 5) & 3
    fy = 2 * zh + (x >> 1)

    where = jnp.stack([((y - fy + a) & 3) * 2 + (c ^ b) for a in range(4) for b in range(2)])
    keep, give = split(amplitudes, where)
    got = send(give, shift(dc=1))
    pieces = weave(c[None], keep, got)
    moved = [send(pieces[a], spread(a)) for a in range(4)]
    moved = [send(moved[a], settle(a)) for a in range(4)]
    own = integrals
    oth = send(integrals, shift(dc=1))
    block = {}
    block[0, 0] = join(jnp.stack([(x - a) & 3 for a in range(4)]), moved)

    block[1, 0] = send(block[0, 0], shift(dx=-1))
    block[3, 0] = send(block[0, 0], shift(dx=1))
    block[0, 1] = send(block[0, 0], shift(dzh=1))
    block[1, 1] = send(block[0, 1], shift(dx=-1))
    block[3, 1] = send(block[0, 1], shift(dx=1))
    parts = {k: (b,) for k, b in block.items()}
    for j in range(2):
        parts[2, j] = (send(block[1, j][:128], shift(dx=-1)), send(block[3, j][128:], shift(dx=1)))

    sums = []
    for group in GROUPS:
        za, zb, one_a, three_b, up, down = product([parts[k] for k in group], own, oth)
        up = send(up, shift(dy=1))
        down = send(down, shift(dy=-1))
        nup = (one_a + up[:, :1024].astype(F32)).astype(BF)
        ndown = (three_b + down[:, 1024:].astype(F32)).astype(BF)
        nup = send(nup, shift(dy=1))
        ndown = send(ndown, shift(dy=-1))
        sums.append((za, zb, up, down, nup, ndown))

    low = (zh == 0).astype(jnp.int32)[None]
    last = []
    for groups, members in LAST:
        stay_a, stay_b, leave_a, leave_b = collect(low, [sums[k] for k in groups], members)
        got_a = send(leave_a, shift(dzl=1))
        got_b = send(leave_b, shift(dzl=1, dc=1))
        stay_b = send(stay_b, shift(dc=1))
        last += [stay_a, got_a, stay_b, got_b]

    slots = partner_slot.reshape(-1)
    mask = tile_mask.reshape(-1)
    order = jnp.argsort(slots, stable=True).astype(jnp.int32)
    inverse = jnp.argsort(order, stable=True).astype(jnp.int32)
    tile_row = jnp.arange(64, dtype=jnp.int32)
    part = ((tile_row >> 4) - x) & 3
    part = (((tile_row >> 3) & 1) ^ c) * 4 + (part ^ (part >> 1))
    row_of = part * 64 + (tile_row & 7) * 8
    tile = jnp.arange(512, dtype=jnp.int32)
    code = ((jnp.repeat(row_of, 8) >> 3) << 4) + ((tile & 7) << 1) + mask
    code = jnp.take(code, order)
    full, out = outgoing(code, *last)
    incoming = lax.all_to_all(out, AXES, split_axis=0, concat_axis=0, tiled=True)
    base, scale = make_base(
        row_of, mask, full, amplitudes, occ_energy[:, None], vir_energy[None, :]
    )
    return update(inverse, incoming.reshape(4096, 128), base, scale)


def solution(mesh):
    in_specs = (
        P("pair", "virt"),
        P("pair", "virt"),
        P("pair"),
        P("virt"),
        P("pair", "virt"),
        P("pair", "virt"),
    )
    out_specs = P("pair", "virt")
    return jax.shard_map(compute, mesh=mesh, in_specs=in_specs, out_specs=out_specs, check_vma=False)
```

```python
import functools
import jax
import jax.numpy as jnp
from jax import lax
from jax.experimental import pallas as pl
from jax.experimental.pallas import tpu as pltpu
from jax.sharding import PartitionSpec as P

AXES = ("pair", "virt")
BF = jnp.bfloat16
F32 = jnp.float32


def decode(device):
    p, v = divmod(device, 16)
    y, zl = divmod(p, 2)
    zh, r = divmod(v, 8)
    x, c = divmod(r, 2)
    return x, y, zl, zh, c


def encode(x, y, zl, zh, c):
    return ((y % 4) * 2 + zl % 2) * 16 + (zh % 2) * 8 + (x % 4) * 2 + c % 2


def permutation(move):
    return [(d, encode(*move(*decode(d)))) for d in range(128)]


def shift(dx=0, dy=0, dzl=0, dzh=0, dc=0):
    return permutation(lambda x, y, zl, zh, c: (x + dx, y + dy, zl + dzl, zh + dzh, c + dc))


def spread(a):
    def move(x, y, zl, zh, c):
        fy, fzl = 2 * zh + x // 2, x % 2
        return (y - fy + a, y, fzl, zl ^ fzl, c)

    return permutation(move)


def settle(a):
    return permutation(lambda x, y, zl, zh, c: (x, y - x + a, zl, zh, c))


def send(value, pairs):
    return lax.ppermute(value, AXES, pairs)


VMEM = pl.BlockSpec(memory_space=pltpu.VMEM)
SMEM = pl.BlockSpec(memory_space=pltpu.SMEM)


def params(megabytes):
    return pltpu.CompilerParams(vmem_limit_bytes=megabytes << 20)


def cost(flops, moved):
    return pl.CostEstimate(flops=flops, bytes_accessed=moved, transcendentals=0)


def split_kernel(where, amp, keep, give):
    for k, out in enumerate((keep, give)):
        for a in range(4):
            row = pl.multiple_of(where[2 * a + k] * 64, 64)
            out[a * 64 : a * 64 + 64, :] = amp[pl.ds(row, 64), :].astype(BF)


def split(amp, where):
    return pl.pallas_call(
        split_kernel,
        out_shape=[jax.ShapeDtypeStruct((256, 1024), BF)] * 2,
        in_specs=[SMEM, VMEM],
        out_specs=[VMEM] * 2,
        compiler_params=params(8),
        cost_estimate=cost(0, 3 << 20),
        name="split",
    )(where, amp)


def weave_kernel(where, keep, got, *outs):
    own = pl.multiple_of(where[0] * 1024, 1024)
    oth = pl.multiple_of(1024 - where[0] * 1024, 1024)
    for a, out in enumerate(outs):
        out[:, pl.ds(own, 1024)] = keep[a * 64 : a * 64 + 64, :]
        out[:, pl.ds(oth, 1024)] = got[a * 64 : a * 64 + 64, :]


def weave(where, keep, got):
    return pl.pallas_call(
        weave_kernel,
        out_shape=[jax.ShapeDtypeStruct((64, 2048), BF)] * 4,
        in_specs=[SMEM] + [VMEM] * 2,
        out_specs=[VMEM] * 4,
        compiler_params=params(6),
        cost_estimate=cost(0, 2 << 20),
        name="weave",
    )(where, keep, got)


def join_kernel(where, *refs):
    out = refs[-1]
    for a in range(4):
        out[pl.ds(pl.multiple_of(where[a] * 64, 64), 64), :] = refs[a][...]


def join(where, pieces):
    return pl.pallas_call(
        join_kernel,
        out_shape=jax.ShapeDtypeStruct((256, 2048), BF),
        in_specs=[SMEM] + [VMEM] * 4,
        out_specs=VMEM,
        compiler_params=params(6),
        cost_estimate=cost(0, 2 << 20),
        name="join",
    )(where, *pieces)


def product_kernel(counts, *refs):
    n_in = sum(counts)
    n = len(counts)
    blocks = refs[:n_in]
    own, oth = refs[n_in : n_in + 2]
    zero_a, zero_b, one_a, three_b, up, down = refs[n_in + 2 : n_in + 8]
    held = refs[n_in + 8]
    step = pl.program_id(0)

    @pl.when(step == 0)
    def _():
        at = 0
        for ref in blocks:
            rows = ref.shape[0]
            held[at : at + rows, :] = ref[...]
            at += rows

    def rows_of(r, i, k):
        return r[i * 256 + k * 64 : i * 256 + k * 64 + 64]

    @pl.when(step < 2)
    def _():
        r = jnp.dot(held[...], own[...], preferred_element_type=F32)
        for i in range(n):
            at = slice(i * 64, i * 64 + 64)
            zero_a[at, :] = rows_of(r, i, 0)
            one_a[at, :] = rows_of(r, i, 1)
            up[at, :] = rows_of(r, i, 2).astype(BF)
            down[at, :] = rows_of(r, i, 3).astype(BF)

    @pl.when(step >= 2)
    def _():
        r = jnp.dot(held[...], oth[...], preferred_element_type=F32)
        for i in range(n):
            at = slice(i * 64, i * 64 + 64)
            zero_b[at, :] = rows_of(r, i, 0)
            up[at, :] = rows_of(r, i, 1).astype(BF)
            down[at, :] = rows_of(r, i, 2).astype(BF)
            three_b[at, :] = rows_of(r, i, 3)


def product(groups, own, oth):
    flat = [a for g in groups for a in g]
    counts = tuple(len(g) for g in groups)
    n = len(groups)
    whole = lambda a: pl.BlockSpec(a.shape, lambda s: (0, 0))
    first = lambda s: (0, jnp.minimum(s, 1))
    second = lambda s: (0, jnp.maximum(s - 2, 0))
    half = jax.ShapeDtypeStruct((n * 64, 1024), F32)
    full = jax.ShapeDtypeStruct((n * 64, 2048), BF)
    out = lambda at: pl.BlockSpec((n * 64, 512), at)
    return pl.pallas_call(
        functools.partial(product_kernel, counts),
        out_shape=[half] * 4 + [full] * 2,
        grid=(4,),
        in_specs=[whole(a) for a in flat]
        + [pl.BlockSpec((2048, 512), first), pl.BlockSpec((2048, 512), second)],
        out_specs=[out(first), out(second), out(first), out(second)]
        + [out(lambda s: (0, s))] * 2,
        scratch_shapes=[pltpu.VMEM((n * 256, 2048), BF)],
        compiler_params=params(24),
        cost_estimate=cost(2 * n * 256 * 2048 * 2048, (9 << 20) + n * (3 << 20)),
        name="product",
    )(*flat, own, oth)


def settle_kernel(n_groups, members, low, *refs):
    ins, outs = refs[: 6 * n_groups], refs[6 * n_groups :]
    stay_a, stay_b, leave_a, leave_b = outs

    def total(g, n):
        za, zb, up, down, nup, ndown = ins[6 * g : 6 * g + 6]
        at = slice(n * 64, n * 64 + 64)
        a = za[at, :] + down[at, :1024].astype(F32) + nup[at, :].astype(F32)
        b = zb[at, :] + up[at, 1024:].astype(F32) + ndown[at, :].astype(F32)
        return a, b

    def write(swap):
        for k, (c0, c1) in enumerate(members):
            at = slice(k * 64, k * 64 + 64)
            a, b = total(*(c1 if swap else c0))
            stay_a[at, :] = a
            stay_b[at, :] = b
            a, b = total(*(c0 if swap else c1))
            leave_a[at, :] = a.astype(BF)
            leave_b[at, :] = b.astype(BF)

    @pl.when(low[0] == 1)
    def _():
        write(False)

    @pl.when(low[0] == 0)
    def _():
        write(True)


def collect(low, groups, members):
    rows = 64 * len(members)
    flat = [a for g in groups for a in g]
    return pl.pallas_call(
        functools.partial(settle_kernel, len(groups), members),
        out_shape=[jax.ShapeDtypeStruct((rows, 1024), F32)] * 2
        + [jax.ShapeDtypeStruct((rows, 1024), BF)] * 2,
        in_specs=[SMEM] + [VMEM] * len(flat),
        out_specs=[VMEM] * 4,
        compiler_params=params(20),
        cost_estimate=cost(0, rows * 1024 * 24),
        name="collect",
    )(low, *flat)


def index_kernel(place, slots, mask, inverse, code, row_of, count):
    x = place[0]
    c = place[1]

    def clear(s, carry):
        count[s] = 0
        return carry

    lax.fori_loop(0, 128, clear, 0, unroll=8)

    def row(r, carry):
        i = lax.bitwise_and(lax.shift_right_logical(r, 4) - x + 4, 3)
        other = lax.bitwise_xor(lax.bitwise_and(lax.shift_right_logical(r, 3), 1), c)
        part = other * 4 + lax.bitwise_xor(i, lax.shift_right_logical(i, 1))
        at = part * 8 + lax.bitwise_and(r, 7)
        row_of[r] = at * 8
        for k in range(8):
            t = r * 8 + k
            s = slots[t]
            n = count[s]
            count[s] = n + 1
            q = s * 4 + n
            inverse[t] = q
            code[q] = at * 16 + k * 2 + mask[t]
        return carry

    lax.fori_loop(0, 64, row, 0)


def index(place, slots, mask):
    return pl.pallas_call(
        index_kernel,
        out_shape=[jax.ShapeDtypeStruct((n,), jnp.int32) for n in (512, 512, 64)],
        in_specs=[SMEM] * 3,
        out_specs=[SMEM] * 3,
        scratch_shapes=[pltpu.SMEM((128,), jnp.int32)],
        compiler_params=params(1),
        cost_estimate=cost(0, 8 << 10),
        name="index",
    )(place, slots, mask)


def outgoing_kernel(code, *refs):
    full, out = refs[-2:]
    at = 0
    for k in (0, 2):
        for g in range(2):
            stay, got = refs[4 * g + k : 4 * g + k + 2]
            rows = stay.shape[0]
            full[at : at + rows, :] = stay[...] + got[...].astype(F32)
            at += rows

    def gather(s, carry):
        rows = []
        for j in range(4):
            q = code[s * 4 + j]
            row = pl.multiple_of(lax.shift_right_logical(q, 4) * 8, 8)
            col = pl.multiple_of(lax.bitwise_and(lax.shift_right_logical(q, 1), 7) * 128, 128)
            w = lax.bitwise_and(q, 1).astype(F32)
            rows.append(full[pl.ds(row, 8), pl.ds(col, 128)] * w)
        out[s] = jnp.concatenate(rows, axis=0).astype(BF)
        return carry

    lax.fori_loop(0, 128, gather, 0, unroll=4)


def outgoing(code, *parts):
    return pl.pallas_call(
        outgoing_kernel,
        out_shape=[
            jax.ShapeDtypeStruct((512, 1024), F32),
            jax.ShapeDtypeStruct((128, 32, 128), BF),
        ],
        in_specs=[SMEM] + [VMEM] * 8,
        out_specs=[VMEM] * 2,
        compiler_params=params(12),
        cost_estimate=cost(0, 6 << 20),
        name="outgoing",
    )(code, *parts)


def base_kernel(row_of, mask, full, amp, occ, vir, base, scale):
    def row(r, carry):
        at = pl.multiple_of(r * 8, 8)
        src = pl.multiple_of(row_of[r], 8)
        e = occ[pl.ds(at, 8), :]
        for k in range(8):
            w = mask[r * 8 + k].astype(F32)
            cols = slice(k * 128, k * 128 + 128)
            q = 1.0 / (e + vir[:, cols])
            scale[pl.ds(at, 8), cols] = q
            base[pl.ds(at, 8), cols] = amp[pl.ds(at, 8), cols] - full[pl.ds(src, 8), cols] * w * q
        return carry

    lax.fori_loop(0, 64, row, 0, unroll=2)


def make_base(row_of, mask, full, amp, occ, vir):
    return pl.pallas_call(
        base_kernel,
        out_shape=[jax.ShapeDtypeStruct((512, 1024), F32)] * 2,
        in_specs=[SMEM] * 2 + [VMEM] * 4,
        out_specs=[VMEM] * 2,
        compiler_params=params(14),
        cost_estimate=cost(0, 8 << 20),
        name="base",
    )(row_of, mask, full, amp, occ, vir)


def update_kernel(inverse, incoming, base, scale, out, wide):
    wide[...] = incoming[...].astype(F32)

    def row(r, carry):
        at = pl.multiple_of(r * 8, 8)
        for k in range(8):
            q = inverse[r * 8 + k]
            partner = wide[pl.ds(pl.multiple_of(q * 8, 8), 8), :]
            cols = slice(k * 128, k * 128 + 128)
            out[pl.ds(at, 8), cols] = base[pl.ds(at, 8), cols] - partner * scale[pl.ds(at, 8), cols]
        return carry

    lax.fori_loop(0, 64, row, 0, unroll=4)


def update(inverse, incoming, base, scale):
    return pl.pallas_call(
        update_kernel,
        out_shape=jax.ShapeDtypeStruct((512, 1024), F32),
        in_specs=[SMEM] + [VMEM] * 3,
        out_specs=VMEM,
        scratch_shapes=[pltpu.VMEM((4096, 128), F32)],
        compiler_params=params(12),
        cost_estimate=cost(0, 7 << 20),
        name="update",
    )(inverse, incoming, base, scale)


GROUPS = (((0, 0),), ((0, 1), (1, 0), (3, 0)), ((1, 1), (3, 1)), ((2, 0), (2, 1)))
LAST = (
    ((0, 1, 2), (((0, 0), (1, 0)), ((1, 1), (2, 0)), ((1, 2), (2, 1)))),
    ((3,), (((0, 0), (0, 1)),)),
)


def compute(amplitudes, integrals, occ_energy, vir_energy, tile_mask, partner_slot):
    device = lax.axis_index(AXES)
    c, x, zh = device & 1, (device >> 1) & 3, (device >> 3) & 1
    y = (device >> 5) & 3
    fy = 2 * zh + (x >> 1)

    where = jnp.stack([((y - fy + a) & 3) * 2 + (c ^ b) for a in range(4) for b in range(2)])
    keep, give = split(amplitudes, where)
    got = send(give, shift(dc=1))
    pieces = weave(c[None], keep, got)
    moved = [send(pieces[a], spread(a)) for a in range(4)]
    moved = [send(moved[a], settle(a)) for a in range(4)]
    own = integrals
    oth = send(integrals, shift(dc=1))
    block = {}
    block[0, 0] = join(jnp.stack([(x - a) & 3 for a in range(4)]), moved)

    block[1, 0] = send(block[0, 0], shift(dx=-1))
    block[3, 0] = send(block[0, 0], shift(dx=1))
    block[0, 1] = send(block[0, 0], shift(dzh=1))
    block[1, 1] = send(block[0, 1], shift(dx=-1))
    block[3, 1] = send(block[0, 1], shift(dx=1))
    parts = {k: (b,) for k, b in block.items()}
    for j in range(2):
        parts[2, j] = (send(block[1, j][:128], shift(dx=-1)), send(block[3, j][128:], shift(dx=1)))

    sums = []
    for group in GROUPS:
        za, zb, one_a, three_b, up, down = product([parts[k] for k in group], own, oth)
        up = send(up, shift(dy=1))
        down = send(down, shift(dy=-1))
        nup = (one_a + up[:, :1024].astype(F32)).astype(BF)
        ndown = (three_b + down[:, 1024:].astype(F32)).astype(BF)
        nup = send(nup, shift(dy=1))
        ndown = send(ndown, shift(dy=-1))
        sums.append((za, zb, up, down, nup, ndown))

    low = (zh == 0).astype(jnp.int32)[None]
    last = []
    for groups, members in LAST:
        stay_a, stay_b, leave_a, leave_b = collect(low, [sums[k] for k in groups], members)
        got_a = send(leave_a, shift(dzl=1))
        got_b = send(leave_b, shift(dzl=1, dc=1))
        stay_b = send(stay_b, shift(dc=1))
        last += [stay_a, got_a, stay_b, got_b]

    mask = tile_mask.reshape(-1)
    inverse, code, row_of = index(jnp.stack([x, c]), partner_slot.reshape(-1), mask)
    full, out = outgoing(code, *last)
    incoming = lax.all_to_all(out, AXES, split_axis=0, concat_axis=0, tiled=True)
    base, scale = make_base(
        row_of, mask, full, amplitudes, occ_energy[:, None], vir_energy[None, :]
    )
    return update(inverse, incoming.reshape(4096, 128), base, scale)


def solution(mesh):
    in_specs = (
        P("pair", "virt"),
        P("pair", "virt"),
        P("pair"),
        P("virt"),
        P("pair", "virt"),
        P("pair", "virt"),
    )
    out_specs = P("pair", "virt")
    return jax.shard_map(compute, mesh=mesh, in_specs=in_specs, out_specs=out_specs, check_vma=False)
```

```python
import functools
import jax
import jax.numpy as jnp
from jax import lax
from jax.experimental import pallas as pl
from jax.experimental.pallas import tpu as pltpu
from jax.sharding import PartitionSpec as P

AXES = ("pair", "virt")
BF = jnp.bfloat16
F32 = jnp.float32


def decode(device):
    p, v = divmod(device, 16)
    y, zl = divmod(p, 2)
    zh, r = divmod(v, 8)
    x, c = divmod(r, 2)
    return x, y, zl, zh, c


def encode(x, y, zl, zh, c):
    return ((y % 4) * 2 + zl % 2) * 16 + (zh % 2) * 8 + (x % 4) * 2 + c % 2


def permutation(move):
    return [(d, encode(*move(*decode(d)))) for d in range(128)]


def shift(dx=0, dy=0, dzl=0, dzh=0, dc=0):
    return permutation(lambda x, y, zl, zh, c: (x + dx, y + dy, zl + dzl, zh + dzh, c + dc))


def spread(a):
    def move(x, y, zl, zh, c):
        fy, fzl = 2 * zh + x // 2, x % 2
        return (y - fy + a, fy, fzl, zl, c)

    return permutation(move)


def send(value, pairs):
    return lax.ppermute(value, AXES, pairs)


VMEM = pl.BlockSpec(memory_space=pltpu.VMEM)
SMEM = pl.BlockSpec(memory_space=pltpu.SMEM)
HBM = pl.BlockSpec(memory_space=pltpu.HBM)
ANY = pl.BlockSpec(memory_space=pl.ANY)


def off_chip(*arrays):
    return [pltpu.with_memory_space_constraint(a, pltpu.HBM) for a in arrays]


def params(megabytes):
    return pltpu.CompilerParams(vmem_limit_bytes=megabytes << 20)


def cost(flops, moved):
    return pl.CostEstimate(flops=flops, bytes_accessed=moved, transcendentals=0)


def split_kernel(where, amp, keep, give):
    for k, out in enumerate((keep, give)):
        for a in range(4):
            row = pl.multiple_of(where[2 * a + k] * 64, 64)
            out[a * 64 : a * 64 + 64, :] = amp[pl.ds(row, 64), :].astype(BF)


def split(amp, where):
    return pl.pallas_call(
        split_kernel,
        out_shape=[jax.ShapeDtypeStruct((256, 1024), BF)] * 2,
        in_specs=[SMEM, VMEM],
        out_specs=[VMEM] * 2,
        compiler_params=params(8),
        cost_estimate=cost(0, 3 << 20),
        name="split",
    )(where, amp)


def weave_kernel(where, keep, got, *outs):
    own = pl.multiple_of(where[0] * 1024, 1024)
    oth = pl.multiple_of(1024 - where[0] * 1024, 1024)
    for a, out in enumerate(outs):
        out[:, pl.ds(own, 1024)] = keep[a * 64 : a * 64 + 64, :]
        out[:, pl.ds(oth, 1024)] = got[a * 64 : a * 64 + 64, :]


def weave(where, keep, got):
    return pl.pallas_call(
        weave_kernel,
        out_shape=[jax.ShapeDtypeStruct((64, 2048), BF)] * 4,
        in_specs=[SMEM] + [VMEM] * 2,
        out_specs=[VMEM] * 4,
        compiler_params=params(6),
        cost_estimate=cost(0, 2 << 20),
        name="weave",
    )(where, keep, got)


def join_kernel(where, *refs):
    out = refs[-1]
    for a in range(4):
        out[pl.ds(pl.multiple_of(where[a] * 64, 64), 64), :] = refs[a][...]


def join(where, pieces):
    return pl.pallas_call(
        join_kernel,
        out_shape=jax.ShapeDtypeStruct((256, 2048), BF),
        in_specs=[SMEM] + [VMEM] * 4,
        out_specs=VMEM,
        compiler_params=params(6),
        cost_estimate=cost(0, 2 << 20),
        name="join",
    )(where, *pieces)


def product_kernel(counts, *refs):
    n_in = sum(counts)
    n = len(counts)
    blocks = refs[:n_in]
    own, oth = refs[n_in : n_in + 2]
    zero_a, zero_b, one_a, three_b, up, down = refs[n_in + 2 : n_in + 8]
    held, keep_a, keep_b, sems = refs[n_in + 8 :]
    at = 0
    for ref in blocks:
        rows = ref.shape[0]
        held[at : at + rows, :] = ref[...]
        at += rows

    def rows_of(r, i, k):
        return r[i * 256 + k * 64 : i * 256 + k * 64 + 64]

    def first(j, carry):
        cols = pl.ds(pl.multiple_of(j * 512, 512), 512)
        r = jnp.dot(held[...], own[:, cols], preferred_element_type=F32)
        for i in range(n):
            at = slice(i * 64, i * 64 + 64)
            keep_a[at, cols] = rows_of(r, i, 0)
            one_a[at, cols] = rows_of(r, i, 1)
            up[at, cols] = rows_of(r, i, 2).astype(BF)
            down[at, cols] = rows_of(r, i, 3).astype(BF)
        return carry

    def second(j, carry):
        cols = pl.ds(pl.multiple_of(j * 512, 512), 512)
        wide = pl.ds(pl.multiple_of(j * 512 + 1024, 512), 512)
        r = jnp.dot(held[...], oth[:, cols], preferred_element_type=F32)
        for i in range(n):
            at = slice(i * 64, i * 64 + 64)
            keep_b[at, cols] = rows_of(r, i, 0)
            up[at, wide] = rows_of(r, i, 1).astype(BF)
            down[at, wide] = rows_of(r, i, 2).astype(BF)
            three_b[at, cols] = rows_of(r, i, 3)
        return carry

    lax.fori_loop(0, 2, first, 0)
    copy_a = pltpu.make_async_copy(keep_a, zero_a, sems.at[0])
    copy_a.start()
    lax.fori_loop(0, 2, second, 0)
    copy_b = pltpu.make_async_copy(keep_b, zero_b, sems.at[1])
    copy_b.start()
    copy_a.wait()
    copy_b.wait()


def product(groups, own, oth):
    flat = [a for g in groups for a in g]
    counts = tuple(len(g) for g in groups)
    n = len(groups)
    half = jax.ShapeDtypeStruct((n * 64, 1024), F32)
    full = jax.ShapeDtypeStruct((n * 64, 2048), BF)
    return pl.pallas_call(
        functools.partial(product_kernel, counts),
        out_shape=[pltpu.HBM(half.shape, F32)] * 2 + [half] * 2 + [full] * 2,
        in_specs=[VMEM] * (len(flat) + 2),
        out_specs=[HBM] * 2 + [VMEM] * 4,
        scratch_shapes=[
            pltpu.VMEM((n * 256, 2048), BF),
            pltpu.VMEM((n * 64, 1024), F32),
            pltpu.VMEM((n * 64, 1024), F32),
            pltpu.SemaphoreType.DMA((2,)),
        ],
        compiler_params=params(28),
        cost_estimate=cost(2 * n * 256 * 2048 * 2048, (9 << 20) + n * (3 << 20)),
        name="product",
    )(*flat, own, oth)


def collect_kernel(n_groups, members, low, *refs):
    ins = refs[: 6 * n_groups]
    stay_a, stay_b, leave_a, leave_b = refs[6 * n_groups : 6 * n_groups + 4]
    wide, thin, sems = refs[6 * n_groups + 4 :]
    chunks = [q for pair in members for q in pair]
    copies = []
    for k, (g, n) in enumerate(chunks):
        za, zb, up, down, nup, ndown = ins[6 * g : 6 * g + 6]
        at = pl.ds(n * 64, 64)
        pairs = (
            (za.at[at, :], wide.at[2 * k]),
            (zb.at[at, :], wide.at[2 * k + 1]),
            (down.at[at, pl.ds(0, 1024)], thin.at[4 * k]),
            (nup.at[at, :], thin.at[4 * k + 1]),
            (up.at[at, pl.ds(1024, 1024)], thin.at[4 * k + 2]),
            (ndown.at[at, :], thin.at[4 * k + 3]),
        )
        copies += [pltpu.make_async_copy(a, b, sems.at[6 * k + j]) for j, (a, b) in enumerate(pairs)]
    for copy in copies:
        copy.start()
    for copy in copies:
        copy.wait()

    def total(k):
        a = wide[2 * k] + thin[4 * k].astype(F32) + thin[4 * k + 1].astype(F32)
        b = wide[2 * k + 1] + thin[4 * k + 2].astype(F32) + thin[4 * k + 3].astype(F32)
        return a, b

    def write(swap):
        for k in range(len(members)):
            at = slice(k * 64, k * 64 + 64)
            a, b = total(2 * k + swap)
            stay_a[at, :] = a
            stay_b[at, :] = b
            a, b = total(2 * k + 1 - swap)
            leave_a[at, :] = a.astype(BF)
            leave_b[at, :] = b.astype(BF)

    @pl.when(low[0] == 1)
    def _():
        write(0)

    @pl.when(low[0] == 0)
    def _():
        write(1)


def collect(low, groups, members):
    rows = 64 * len(members)
    flat = []
    for g in groups:
        flat += off_chip(*g[:2]) + (off_chip(*g[2:]) if len(groups) > 1 else list(g[2:]))
    n = 2 * len(members)
    return pl.pallas_call(
        functools.partial(collect_kernel, len(groups), members),
        out_shape=[jax.ShapeDtypeStruct((rows, 1024), F32)] * 2
        + [jax.ShapeDtypeStruct((rows, 1024), BF)] * 2,
        in_specs=[SMEM] + [ANY] * len(flat),
        out_specs=[VMEM] * 4,
        scratch_shapes=[
            pltpu.VMEM((2 * n, 64, 1024), F32),
            pltpu.VMEM((4 * n, 64, 1024), BF),
            pltpu.SemaphoreType.DMA((6 * n,)),
        ],
        compiler_params=params(12),
        cost_estimate=cost(0, rows * 1024 * 24),
        name="collect",
    )(low, *flat)


def index_kernel(place, slots, mask, inverse, code, row_of, count):
    x = place[0]
    c = place[1]

    def clear(s, carry):
        count[s] = 0
        return carry

    lax.fori_loop(0, 128, clear, 0, unroll=8)

    def row(r, carry):
        i = lax.bitwise_and(lax.shift_right_logical(r, 4) - x + 4, 3)
        other = lax.bitwise_xor(lax.bitwise_and(lax.shift_right_logical(r, 3), 1), c)
        part = other * 4 + lax.bitwise_xor(i, lax.shift_right_logical(i, 1))
        at = part * 8 + lax.bitwise_and(r, 7)
        row_of[r] = at * 8
        for k in range(8):
            t = r * 8 + k
            s = slots[t]
            n = count[s]
            count[s] = n + 1
            q = s * 4 + n
            inverse[t] = q
            code[q] = at * 16 + k * 2 + mask[t]
        return carry

    lax.fori_loop(0, 64, row, 0)


def index(place, slots, mask):
    return pl.pallas_call(
        index_kernel,
        out_shape=[jax.ShapeDtypeStruct((n,), jnp.int32) for n in (512, 512, 64)],
        in_specs=[SMEM] * 3,
        out_specs=[SMEM] * 3,
        scratch_shapes=[pltpu.SMEM((128,), jnp.int32)],
        compiler_params=params(1),
        cost_estimate=cost(0, 8 << 10),
        name="index",
    )(place, slots, mask)


def outgoing_kernel(code, *refs):
    ins = refs[:12]
    full, out = refs[12:14]
    full_v, out_v, wide, thin, sems = refs[14:]
    copies = []
    at = 0
    for k in (0, 2):
        for g in range(2):
            stay, got = ins[4 * g + k : 4 * g + k + 2]
            rows = stay.shape[0]
            n = len(copies)
            copies += [
                pltpu.make_async_copy(stay, wide.at[pl.ds(at, rows), :], sems.at[n]),
                pltpu.make_async_copy(got, thin.at[pl.ds(at, rows), :], sems.at[n + 1]),
            ]
            at += rows
    for copy in copies:
        copy.start()
    for k, to in ((0, 192), (2, 448)):
        stay, got = ins[8 + k : 8 + k + 2]
        full_v[to : to + 64, :] = stay[...] + got[...].astype(F32)
    for copy in copies:
        copy.wait()
    for at, to in ((0, 0), (192, 256)):
        full_v[to : to + 192, :] = wide[at : at + 192, :] + thin[at : at + 192, :].astype(F32)
    save = pltpu.make_async_copy(full_v, full, sems.at[8])
    save.start()

    def gather(s, carry):
        rows = []
        for j in range(4):
            q = code[s * 4 + j]
            row = pl.multiple_of(lax.shift_right_logical(q, 4) * 8, 8)
            col = pl.multiple_of(lax.bitwise_and(lax.shift_right_logical(q, 1), 7) * 128, 128)
            w = lax.bitwise_and(q, 1).astype(F32)
            rows.append(full_v[pl.ds(row, 8), pl.ds(col, 128)] * w)
        out_v[s] = jnp.concatenate(rows, axis=0).astype(BF)
        return carry

    sends = []
    for k in range(4):
        part = pl.ds(32 * k, 32)
        lax.fori_loop(32 * k, 32 * k + 32, gather, 0, unroll=4)
        sends.append(pltpu.make_async_copy(out_v.at[part], out.at[part], sems.at[9 + k]))
        sends[-1].start()
    for copy in sends:
        copy.wait()
    save.wait()


def outgoing(code, *parts):
    return pl.pallas_call(
        outgoing_kernel,
        out_shape=[pltpu.HBM((512, 1024), F32), pltpu.HBM((128, 32, 128), BF)],
        in_specs=[SMEM] + [ANY] * 8 + [VMEM] * 4,
        out_specs=[HBM] * 2,
        scratch_shapes=[
            pltpu.VMEM((512, 1024), F32),
            pltpu.VMEM((128, 32, 128), BF),
            pltpu.VMEM((384, 1024), F32),
            pltpu.VMEM((384, 1024), BF),
            pltpu.SemaphoreType.DMA((13,)),
        ],
        compiler_params=params(12),
        cost_estimate=cost(0, 6 << 20),
        name="outgoing",
    )(code, *parts)


def base_kernel(row_of, mask, full, amp, occ, vir, base, scale):
    def row(r, carry):
        at = pl.multiple_of(r * 8, 8)
        src = pl.multiple_of(row_of[r], 8)
        e = occ[pl.ds(at, 8), :]
        for k in range(8):
            w = mask[r * 8 + k].astype(F32)
            cols = slice(k * 128, k * 128 + 128)
            q = 1.0 / (e + vir[:, cols])
            scale[pl.ds(at, 8), cols] = q
            base[pl.ds(at, 8), cols] = amp[pl.ds(at, 8), cols] - full[pl.ds(src, 8), cols] * w * q
        return carry

    lax.fori_loop(0, 64, row, 0, unroll=2)


def make_base(row_of, mask, full, amp, occ, vir):
    return pl.pallas_call(
        base_kernel,
        out_shape=[jax.ShapeDtypeStruct((512, 1024), F32)] * 2,
        in_specs=[SMEM] * 2 + [VMEM] * 4,
        out_specs=[VMEM] * 2,
        compiler_params=params(14),
        cost_estimate=cost(0, 8 << 20),
        name="base",
    )(row_of, mask, full, amp, occ, vir)


def update_kernel(inverse, incoming, base, scale, out, wide, base_v, scale_v, out_v, sems):
    loads = []
    for k in range(4):
        part = pl.ds(128 * k, 128)
        loads.append(
            (
                pltpu.make_async_copy(base.at[part, :], base_v.at[part, :], sems.at[3 * k]),
                pltpu.make_async_copy(scale.at[part, :], scale_v.at[part, :], sems.at[3 * k + 1]),
            )
        )
    for pair in loads:
        for copy in pair:
            copy.start()
    wide[...] = incoming[...].astype(F32)

    def row(r, carry):
        at = pl.multiple_of(r * 8, 8)
        for k in range(8):
            q = inverse[r * 8 + k]
            partner = wide[pl.ds(pl.multiple_of(q * 8, 8), 8), :]
            cols = slice(k * 128, k * 128 + 128)
            out_v[pl.ds(at, 8), cols] = (
                base_v[pl.ds(at, 8), cols] - partner * scale_v[pl.ds(at, 8), cols]
            )
        return carry

    stores = []
    for k in range(4):
        for copy in loads[k]:
            copy.wait()
        lax.fori_loop(16 * k, 16 * k + 16, row, 0, unroll=4)
        part = pl.ds(128 * k, 128)
        stores.append(pltpu.make_async_copy(out_v.at[part, :], out.at[part, :], sems.at[3 * k + 2]))
        stores[-1].start()
    for copy in stores:
        copy.wait()


def update(inverse, incoming, base, scale):
    return pl.pallas_call(
        update_kernel,
        out_shape=jax.ShapeDtypeStruct((512, 1024), F32),
        in_specs=[SMEM, VMEM, HBM, HBM],
        out_specs=HBM,
        scratch_shapes=[
            pltpu.VMEM((4096, 128), F32),
            pltpu.VMEM((512, 1024), F32),
            pltpu.VMEM((512, 1024), F32),
            pltpu.VMEM((512, 1024), F32),
            pltpu.SemaphoreType.DMA((12,)),
        ],
        compiler_params=params(14),
        cost_estimate=cost(0, 7 << 20),
        name="update",
    )(inverse, incoming, *off_chip(base, scale))


GROUPS = (((0, 0),), ((0, 1), (1, 0), (3, 0)), ((1, 1), (3, 1)), ((2, 0), (2, 1)))
LAST = (
    ((0, 1), (((0, 0), (1, 0)),)),
    ((1, 2), (((0, 1), (1, 0)), ((0, 2), (1, 1)))),
    ((3,), (((0, 0), (0, 1)),)),
)


def compute(amplitudes, integrals, occ_energy, vir_energy, tile_mask, partner_slot):
    device = lax.axis_index(AXES)
    c, x, zh = device & 1, (device >> 1) & 3, (device >> 3) & 1
    y = (device >> 5) & 3
    fy = 2 * zh + (x >> 1)

    where = jnp.stack([((y - fy + a) & 3) * 2 + (c ^ b) for a in range(4) for b in range(2)])
    keep, give = split(amplitudes, where)
    got = send(give, shift(dc=1))
    pieces = weave(c[None], keep, got)
    moved = [send(pieces[a], spread(a)) for a in range(4)]
    own = integrals
    oth = send(integrals, shift(dc=1))
    block = {}
    block[0, 0] = join(jnp.stack([(x - a) & 3 for a in range(4)]), moved)

    block[1, 0] = send(block[0, 0], shift(dx=-1))
    block[3, 0] = send(block[0, 0], shift(dx=1))
    block[0, 1] = send(block[0, 0], shift(dzh=1))
    block[1, 1] = send(block[0, 1], shift(dx=-1))
    block[3, 1] = send(block[0, 1], shift(dx=1))
    parts = {k: (b,) for k, b in block.items()}
    for j in range(2):
        parts[2, j] = (send(block[1, j][:128], shift(dx=-1)), send(block[3, j][128:], shift(dx=1)))

    sums = []
    for group in GROUPS:
        za, zb, one_a, three_b, up, down = product([parts[k] for k in group], own, oth)
        up = send(up, shift(dy=1))
        down = send(down, shift(dy=-1))
        nup = (one_a + up[:, :1024].astype(F32)).astype(BF)
        ndown = (three_b + down[:, 1024:].astype(F32)).astype(BF)
        nup = send(nup, shift(dy=1))
        ndown = send(ndown, shift(dy=-1))
        sums.append((za, zb, up, down, nup, ndown))

    low = (zh == ((device >> 4) & 1)).astype(jnp.int32)[None]
    last = []
    for groups, members in LAST:
        stay_a, stay_b, leave_a, leave_b = collect(low, [sums[k] for k in groups], members)
        got_a = send(leave_a, shift(dzl=1))
        got_b = send(leave_b, shift(dzl=1, dc=1))
        stay_b = send(stay_b, shift(dc=1))
        last += [stay_a, got_a, stay_b, got_b]

    mask = tile_mask.reshape(-1)
    inverse, code, row_of = index(jnp.stack([x, c]), partner_slot.reshape(-1), mask)
    full, out = outgoing(code, *last)
    incoming = lax.all_to_all(out, AXES, split_axis=0, concat_axis=0, tiled=True)
    base, scale = make_base(
        row_of, mask, full, amplitudes, occ_energy[:, None], vir_energy[None, :]
    )
    return update(inverse, incoming.reshape(4096, 128), base, scale)


def solution(mesh):
    in_specs = (
        P("pair", "virt"),
        P("pair", "virt"),
        P("pair"),
        P("virt"),
        P("pair", "virt"),
        P("pair", "virt"),
    )
    out_specs = P("pair", "virt")
    return jax.shard_map(compute, mesh=mesh, in_specs=in_specs, out_specs=out_specs, check_vma=False)
```

```python
import functools
import jax
import jax.numpy as jnp
from jax import lax
from jax.experimental import pallas as pl
from jax.experimental.pallas import tpu as pltpu
from jax.sharding import PartitionSpec as P

AXES = ("pair", "virt")
BF = jnp.bfloat16
F32 = jnp.float32


def decode(device):
    p, v = divmod(device, 16)
    y, zl = divmod(p, 2)
    zh, r = divmod(v, 8)
    x, c = divmod(r, 2)
    return x, y, zl, zh, c


def encode(x, y, zl, zh, c):
    return ((y % 4) * 2 + zl % 2) * 16 + (zh % 2) * 8 + (x % 4) * 2 + c % 2


def permutation(move):
    return [(d, encode(*move(*decode(d)))) for d in range(128)]


def shift(dx=0, dy=0, dzl=0, dzh=0, dc=0):
    return permutation(lambda x, y, zl, zh, c: (x + dx, y + dy, zl + dzl, zh + dzh, c + dc))


def spread(a):
    def move(x, y, zl, zh, c):
        fy, fzl = 2 * zh + x // 2, x % 2
        return (y - fy + a, fy, fzl, zl, c)

    return permutation(move)


def send(value, pairs):
    return lax.ppermute(value, AXES, pairs)


VMEM = pl.BlockSpec(memory_space=pltpu.VMEM)
SMEM = pl.BlockSpec(memory_space=pltpu.SMEM)
HBM = pl.BlockSpec(memory_space=pltpu.HBM)
ANY = pl.BlockSpec(memory_space=pl.ANY)


def off_chip(*arrays):
    return [pltpu.with_memory_space_constraint(a, pltpu.HBM) for a in arrays]


def params(megabytes):
    return pltpu.CompilerParams(vmem_limit_bytes=megabytes << 20)


def cost(flops, moved):
    return pl.CostEstimate(flops=flops, bytes_accessed=moved, transcendentals=0)


def split_kernel(where, amp, keep, give):
    for k, out in enumerate((keep, give)):
        for a in range(4):
            row = pl.multiple_of(where[2 * a + k] * 64, 64)
            out[a * 64 : a * 64 + 64, :] = amp[pl.ds(row, 64), :].astype(BF)


def split(amp, where):
    return pl.pallas_call(
        split_kernel,
        out_shape=[jax.ShapeDtypeStruct((256, 1024), BF)] * 2,
        in_specs=[SMEM, VMEM],
        out_specs=[VMEM] * 2,
        compiler_params=params(8),
        cost_estimate=cost(0, 3 << 20),
        name="split",
    )(where, amp)


def weave_kernel(where, keep, got, *outs):
    own = pl.multiple_of(where[0] * 1024, 1024)
    oth = pl.multiple_of(1024 - where[0] * 1024, 1024)
    for a, out in enumerate(outs):
        out[:, pl.ds(own, 1024)] = keep[a * 64 : a * 64 + 64, :]
        out[:, pl.ds(oth, 1024)] = got[a * 64 : a * 64 + 64, :]


def weave(where, keep, got):
    return pl.pallas_call(
        weave_kernel,
        out_shape=[jax.ShapeDtypeStruct((64, 2048), BF)] * 4,
        in_specs=[SMEM] + [VMEM] * 2,
        out_specs=[VMEM] * 4,
        compiler_params=params(6),
        cost_estimate=cost(0, 2 << 20),
        name="weave",
    )(where, keep, got)


def join_kernel(where, *refs):
    out = refs[-1]
    for a in range(4):
        out[pl.ds(pl.multiple_of(where[a] * 64, 64), 64), :] = refs[a][...]


def join(where, pieces):
    return pl.pallas_call(
        join_kernel,
        out_shape=jax.ShapeDtypeStruct((256, 2048), BF),
        in_specs=[SMEM] + [VMEM] * 4,
        out_specs=VMEM,
        compiler_params=params(6),
        cost_estimate=cost(0, 2 << 20),
        name="join",
    )(where, *pieces)


def hold_kernel(source, target, sem):
    copy = pltpu.make_async_copy(source, target, sem)
    copy.start()
    copy.wait()


def hold(source):
    return pl.pallas_call(
        hold_kernel,
        out_shape=jax.ShapeDtypeStruct(source.shape, source.dtype),
        in_specs=[ANY],
        out_specs=VMEM,
        scratch_shapes=[pltpu.SemaphoreType.DMA],
        compiler_params=params(6),
        cost_estimate=cost(0, 8 << 20),
        name="hold",
    )(*off_chip(source))


def product_kernel(counts, *refs):
    n_in = sum(counts)
    n = len(counts)
    blocks = refs[:n_in]
    own, oth = refs[n_in : n_in + 2]
    zero_a, zero_b, one_a, three_b, up, down = refs[n_in + 2 : n_in + 8]
    held, keep_a, keep_b, sems = refs[n_in + 8 :]
    at = 0
    for ref in blocks:
        rows = ref.shape[0]
        held[at : at + rows, :] = ref[...]
        at += rows

    def rows_of(r, i, k):
        return r[i * 256 + k * 64 : i * 256 + k * 64 + 64]

    def first(j, carry):
        cols = pl.ds(pl.multiple_of(j * 512, 512), 512)
        r = jnp.dot(held[...], own[:, cols], preferred_element_type=F32)
        for i in range(n):
            at = slice(i * 64, i * 64 + 64)
            keep_a[at, cols] = rows_of(r, i, 0)
            one_a[at, cols] = rows_of(r, i, 1)
            up[at, cols] = rows_of(r, i, 2).astype(BF)
            down[at, cols] = rows_of(r, i, 3).astype(BF)
        return carry

    def second(j, carry):
        cols = pl.ds(pl.multiple_of(j * 512, 512), 512)
        wide = pl.ds(pl.multiple_of(j * 512 + 1024, 512), 512)
        r = jnp.dot(held[...], oth[:, cols], preferred_element_type=F32)
        for i in range(n):
            at = slice(i * 64, i * 64 + 64)
            keep_b[at, cols] = rows_of(r, i, 0)
            up[at, wide] = rows_of(r, i, 1).astype(BF)
            down[at, wide] = rows_of(r, i, 2).astype(BF)
            three_b[at, cols] = rows_of(r, i, 3)
        return carry

    lax.fori_loop(0, 2, first, 0)
    copy_a = pltpu.make_async_copy(keep_a, zero_a, sems.at[0])
    copy_a.start()
    lax.fori_loop(0, 2, second, 0)
    copy_b = pltpu.make_async_copy(keep_b, zero_b, sems.at[1])
    copy_b.start()
    copy_a.wait()
    copy_b.wait()


def product(groups, own, oth):
    flat = [a for g in groups for a in g]
    counts = tuple(len(g) for g in groups)
    n = len(groups)
    half = jax.ShapeDtypeStruct((n * 64, 1024), F32)
    full = jax.ShapeDtypeStruct((n * 64, 2048), BF)
    return pl.pallas_call(
        functools.partial(product_kernel, counts),
        out_shape=[pltpu.HBM(half.shape, F32)] * 2 + [half] * 2 + [full] * 2,
        in_specs=[VMEM] * (len(flat) + 2),
        out_specs=[HBM] * 2 + [VMEM] * 4,
        scratch_shapes=[
            pltpu.VMEM((n * 256, 2048), BF),
            pltpu.VMEM((n * 64, 1024), F32),
            pltpu.VMEM((n * 64, 1024), F32),
            pltpu.SemaphoreType.DMA((2,)),
        ],
        compiler_params=params(28),
        cost_estimate=cost(2 * n * 256 * 2048 * 2048, (9 << 20) + n * (3 << 20)),
        name="product",
    )(*flat, own, oth)


def collect_kernel(n_groups, members, low, *refs):
    ins = refs[: 6 * n_groups]
    stay_a, stay_b, leave_a, leave_b = refs[6 * n_groups : 6 * n_groups + 4]
    wide, thin, sems = refs[6 * n_groups + 4 :]
    chunks = [q for pair in members for q in pair]
    copies = []
    for k, (g, n) in enumerate(chunks):
        za, zb, up, down, nup, ndown = ins[6 * g : 6 * g + 6]
        at = pl.ds(n * 64, 64)
        pairs = (
            (za.at[at, :], wide.at[2 * k]),
            (zb.at[at, :], wide.at[2 * k + 1]),
            (down.at[at, pl.ds(0, 1024)], thin.at[4 * k]),
            (nup.at[at, :], thin.at[4 * k + 1]),
            (up.at[at, pl.ds(1024, 1024)], thin.at[4 * k + 2]),
            (ndown.at[at, :], thin.at[4 * k + 3]),
        )
        copies += [pltpu.make_async_copy(a, b, sems.at[6 * k + j]) for j, (a, b) in enumerate(pairs)]
    for copy in copies:
        copy.start()
    for copy in copies:
        copy.wait()

    def total(k):
        a = wide[2 * k] + thin[4 * k].astype(F32) + thin[4 * k + 1].astype(F32)
        b = wide[2 * k + 1] + thin[4 * k + 2].astype(F32) + thin[4 * k + 3].astype(F32)
        return a, b

    def write(swap):
        for k in range(len(members)):
            at = slice(k * 64, k * 64 + 64)
            a, b = total(2 * k + swap)
            stay_a[at, :] = a
            stay_b[at, :] = b
            a, b = total(2 * k + 1 - swap)
            leave_a[at, :] = a.astype(BF)
            leave_b[at, :] = b.astype(BF)

    @pl.when(low[0] == 1)
    def _():
        write(0)

    @pl.when(low[0] == 0)
    def _():
        write(1)


def collect(low, groups, members):
    rows = 64 * len(members)
    flat = []
    for g in groups:
        flat += off_chip(*g[:2]) + (off_chip(*g[2:]) if len(groups) > 1 else list(g[2:]))
    n = 2 * len(members)
    return pl.pallas_call(
        functools.partial(collect_kernel, len(groups), members),
        out_shape=[jax.ShapeDtypeStruct((rows, 1024), F32)] * 2
        + [jax.ShapeDtypeStruct((rows, 1024), BF)] * 2,
        in_specs=[SMEM] + [ANY] * len(flat),
        out_specs=[VMEM] * 4,
        scratch_shapes=[
            pltpu.VMEM((2 * n, 64, 1024), F32),
            pltpu.VMEM((4 * n, 64, 1024), BF),
            pltpu.SemaphoreType.DMA((6 * n,)),
        ],
        compiler_params=params(12),
        cost_estimate=cost(0, rows * 1024 * 24),
        name="collect",
    )(low, *flat)


def index_kernel(place, slots, mask, inverse, code, row_of, count):
    x = place[0]
    c = place[1]

    def clear(s, carry):
        count[s] = 0
        return carry

    lax.fori_loop(0, 128, clear, 0, unroll=8)

    def row(r, carry):
        i = lax.bitwise_and(lax.shift_right_logical(r, 4) - x + 4, 3)
        other = lax.bitwise_xor(lax.bitwise_and(lax.shift_right_logical(r, 3), 1), c)
        part = other * 4 + lax.bitwise_xor(i, lax.shift_right_logical(i, 1))
        at = part * 8 + lax.bitwise_and(r, 7)
        row_of[r] = at * 8
        for k in range(8):
            t = r * 8 + k
            s = slots[t]
            n = count[s]
            count[s] = n + 1
            q = s * 4 + n
            inverse[t] = q
            code[q] = at * 16 + k * 2 + mask[t]
        return carry

    lax.fori_loop(0, 64, row, 0)


def index(place, slots, mask):
    return pl.pallas_call(
        index_kernel,
        out_shape=[jax.ShapeDtypeStruct((n,), jnp.int32) for n in (512, 512, 64)],
        in_specs=[SMEM] * 3,
        out_specs=[SMEM] * 3,
        scratch_shapes=[pltpu.SMEM((128,), jnp.int32)],
        compiler_params=params(1),
        cost_estimate=cost(0, 8 << 10),
        name="index",
    )(place, slots, mask)


def outgoing_kernel(code, *refs):
    ins = refs[:12]
    full, out = refs[12:14]
    full_v, out_v, wide, thin, sems = refs[14:]
    copies = []
    at = 0
    for k in (0, 2):
        for g in range(2):
            stay, got = ins[4 * g + k : 4 * g + k + 2]
            rows = stay.shape[0]
            n = len(copies)
            copies += [
                pltpu.make_async_copy(stay, wide.at[pl.ds(at, rows), :], sems.at[n]),
                pltpu.make_async_copy(got, thin.at[pl.ds(at, rows), :], sems.at[n + 1]),
            ]
            at += rows
    for copy in copies:
        copy.start()
    for k, to in ((0, 192), (2, 448)):
        stay, got = ins[8 + k : 8 + k + 2]
        full_v[to : to + 64, :] = stay[...] + got[...].astype(F32)
    for copy in copies:
        copy.wait()
    for at, to in ((0, 0), (192, 256)):
        full_v[to : to + 192, :] = wide[at : at + 192, :] + thin[at : at + 192, :].astype(F32)
    save = pltpu.make_async_copy(full_v, full, sems.at[8])
    save.start()

    def gather(s, carry):
        rows = []
        for j in range(4):
            q = code[s * 4 + j]
            row = pl.multiple_of(lax.shift_right_logical(q, 4) * 8, 8)
            col = pl.multiple_of(lax.bitwise_and(lax.shift_right_logical(q, 1), 7) * 128, 128)
            w = lax.bitwise_and(q, 1).astype(F32)
            rows.append(full_v[pl.ds(row, 8), pl.ds(col, 128)] * w)
        out_v[s] = jnp.concatenate(rows, axis=0).astype(BF)
        return carry

    sends = []
    for k in range(4):
        part = pl.ds(32 * k, 32)
        lax.fori_loop(32 * k, 32 * k + 32, gather, 0, unroll=4)
        sends.append(pltpu.make_async_copy(out_v.at[part], out.at[part], sems.at[9 + k]))
        sends[-1].start()
    for copy in sends:
        copy.wait()
    save.wait()


def outgoing(code, *parts):
    return pl.pallas_call(
        outgoing_kernel,
        out_shape=[pltpu.HBM((512, 1024), F32), pltpu.HBM((128, 32, 128), BF)],
        in_specs=[SMEM] + [ANY] * 8 + [VMEM] * 4,
        out_specs=[HBM] * 2,
        scratch_shapes=[
            pltpu.VMEM((512, 1024), F32),
            pltpu.VMEM((128, 32, 128), BF),
            pltpu.VMEM((384, 1024), F32),
            pltpu.VMEM((384, 1024), BF),
            pltpu.SemaphoreType.DMA((13,)),
        ],
        compiler_params=params(12),
        cost_estimate=cost(0, 6 << 20),
        name="outgoing",
    )(code, *parts)


def base_kernel(row_of, mask, full, amp, occ, vir, base, scale):
    def row(r, carry):
        at = pl.multiple_of(r * 8, 8)
        src = pl.multiple_of(row_of[r], 8)
        e = occ[pl.ds(at, 8), :]
        for k in range(8):
            w = mask[r * 8 + k].astype(F32)
            cols = slice(k * 128, k * 128 + 128)
            q = 1.0 / (e + vir[:, cols])
            scale[pl.ds(at, 8), cols] = q
            base[pl.ds(at, 8), cols] = amp[pl.ds(at, 8), cols] - full[pl.ds(src, 8), cols] * w * q
        return carry

    lax.fori_loop(0, 64, row, 0, unroll=2)


def make_base(row_of, mask, full, amp, occ, vir):
    return pl.pallas_call(
        base_kernel,
        out_shape=[jax.ShapeDtypeStruct((512, 1024), F32)] * 2,
        in_specs=[SMEM] * 2 + [VMEM] * 4,
        out_specs=[VMEM] * 2,
        compiler_params=params(14),
        cost_estimate=cost(0, 8 << 20),
        name="base",
    )(row_of, mask, full, amp, occ, vir)


def update_kernel(inverse, incoming, base, scale, out, wide, base_v, scale_v, out_v, sems):
    loads = []
    for k in range(4):
        part = pl.ds(128 * k, 128)
        loads.append(
            (
                pltpu.make_async_copy(base.at[part, :], base_v.at[part, :], sems.at[3 * k]),
                pltpu.make_async_copy(scale.at[part, :], scale_v.at[part, :], sems.at[3 * k + 1]),
            )
        )
    for pair in loads:
        for copy in pair:
            copy.start()
    wide[...] = incoming[...].astype(F32)

    def row(r, carry):
        at = pl.multiple_of(r * 8, 8)
        for k in range(8):
            q = inverse[r * 8 + k]
            partner = wide[pl.ds(pl.multiple_of(q * 8, 8), 8), :]
            cols = slice(k * 128, k * 128 + 128)
            out_v[pl.ds(at, 8), cols] = (
                base_v[pl.ds(at, 8), cols] - partner * scale_v[pl.ds(at, 8), cols]
            )
        return carry

    stores = []
    for k in range(4):
        for copy in loads[k]:
            copy.wait()
        lax.fori_loop(16 * k, 16 * k + 16, row, 0, unroll=4)
        part = pl.ds(128 * k, 128)
        stores.append(pltpu.make_async_copy(out_v.at[part, :], out.at[part, :], sems.at[3 * k + 2]))
        stores[-1].start()
    for copy in stores:
        copy.wait()


def update(inverse, incoming, base, scale):
    return pl.pallas_call(
        update_kernel,
        out_shape=jax.ShapeDtypeStruct((512, 1024), F32),
        in_specs=[SMEM, VMEM, HBM, HBM],
        out_specs=HBM,
        scratch_shapes=[
            pltpu.VMEM((4096, 128), F32),
            pltpu.VMEM((512, 1024), F32),
            pltpu.VMEM((512, 1024), F32),
            pltpu.VMEM((512, 1024), F32),
            pltpu.SemaphoreType.DMA((12,)),
        ],
        compiler_params=params(14),
        cost_estimate=cost(0, 7 << 20),
        name="update",
    )(inverse, incoming, *off_chip(base, scale))


GROUPS = (((0, 0),), ((0, 1), (1, 0), (3, 0)), ((1, 1), (3, 1)), ((2, 0), (2, 1)))
LAST = (
    ((0, 1), (((0, 0), (1, 0)),)),
    ((1, 2), (((0, 1), (1, 0)), ((0, 2), (1, 1)))),
    ((3,), (((0, 0), (0, 1)),)),
)


def compute(amplitudes, integrals, occ_energy, vir_energy, tile_mask, partner_slot):
    device = lax.axis_index(AXES)
    c, x, zh = device & 1, (device >> 1) & 3, (device >> 3) & 1
    y = (device >> 5) & 3
    fy = 2 * zh + (x >> 1)

    where = jnp.stack([((y - fy + a) & 3) * 2 + (c ^ b) for a in range(4) for b in range(2)])
    keep, give = split(amplitudes, where)
    got = send(give, shift(dc=1))
    pieces = weave(c[None], keep, got)
    moved = [send(pieces[a], spread(a)) for a in range(4)]
    own = hold(integrals)
    oth = send(integrals, shift(dc=1))
    block = {}
    block[0, 0] = join(jnp.stack([(x - a) & 3 for a in range(4)]), moved)

    block[1, 0] = send(block[0, 0], shift(dx=-1))
    block[3, 0] = send(block[0, 0], shift(dx=1))
    block[0, 1] = send(block[0, 0], shift(dzh=1))
    block[1, 1] = send(block[0, 1], shift(dx=-1))
    block[3, 1] = send(block[0, 1], shift(dx=1))
    parts = {k: (b,) for k, b in block.items()}
    for j in range(2):
        parts[2, j] = (send(block[1, j][:128], shift(dx=-1)), send(block[3, j][128:], shift(dx=1)))

    sums = []
    for group in GROUPS:
        za, zb, one_a, three_b, up, down = product([parts[k] for k in group], own, oth)
        up = send(up, shift(dy=1))
        down = send(down, shift(dy=-1))
        nup = (one_a + up[:, :1024].astype(F32)).astype(BF)
        ndown = (three_b + down[:, 1024:].astype(F32)).astype(BF)
        nup = send(nup, shift(dy=1))
        ndown = send(ndown, shift(dy=-1))
        sums.append((za, zb, up, down, nup, ndown))

    low = (zh == ((device >> 4) & 1)).astype(jnp.int32)[None]
    last = []
    for groups, members in LAST:
        stay_a, stay_b, leave_a, leave_b = collect(low, [sums[k] for k in groups], members)
        got_a = send(leave_a, shift(dzl=1))
        got_b = send(leave_b, shift(dzl=1, dc=1))
        stay_b = send(stay_b, shift(dc=1))
        last += [stay_a, got_a, stay_b, got_b]

    mask = tile_mask.reshape(-1)
    inverse, code, row_of = index(jnp.stack([x, c]), partner_slot.reshape(-1), mask)
    full, out = outgoing(code, *last)
    incoming = lax.all_to_all(out, AXES, split_axis=0, concat_axis=0, tiled=True)
    base, scale = make_base(
        row_of, mask, full, amplitudes, occ_energy[:, None], vir_energy[None, :]
    )
    return update(inverse, incoming.reshape(4096, 128), base, scale)


def solution(mesh):
    in_specs = (
        P("pair", "virt"),
        P("pair", "virt"),
        P("pair"),
        P("virt"),
        P("pair", "virt"),
        P("pair", "virt"),
    )
    out_specs = P("pair", "virt")
    return jax.shard_map(compute, mesh=mesh, in_specs=in_specs, out_specs=out_specs, check_vma=False)
```

```python
import functools
import jax
import jax.numpy as jnp
from jax import lax
from jax.experimental import pallas as pl
from jax.experimental.pallas import tpu as pltpu
from jax.sharding import PartitionSpec as P

AXES = ("pair", "virt")
BF = jnp.bfloat16
F32 = jnp.float32


def decode(device):
    p, v = divmod(device, 16)
    y, zl = divmod(p, 2)
    zh, r = divmod(v, 8)
    x, c = divmod(r, 2)
    return x, y, zl, zh, c


def encode(x, y, zl, zh, c):
    return ((y % 4) * 2 + zl % 2) * 16 + (zh % 2) * 8 + (x % 4) * 2 + c % 2


def permutation(move):
    return [(d, encode(*move(*decode(d)))) for d in range(128)]


def shift(dx=0, dy=0, dzl=0, dzh=0, dc=0):
    return permutation(lambda x, y, zl, zh, c: (x + dx, y + dy, zl + dzl, zh + dzh, c + dc))


def spread(a):
    def move(x, y, zl, zh, c):
        fy, fzl = 2 * zh + x // 2, x % 2
        return (y - fy + a, fy, fzl, zl, c)

    return permutation(move)


def send(value, pairs):
    return lax.ppermute(value, AXES, pairs)


VMEM = pl.BlockSpec(memory_space=pltpu.VMEM)
SMEM = pl.BlockSpec(memory_space=pltpu.SMEM)
HBM = pl.BlockSpec(memory_space=pltpu.HBM)
ANY = pl.BlockSpec(memory_space=pl.ANY)


def off_chip(*arrays):
    return [pltpu.with_memory_space_constraint(a, pltpu.HBM) for a in arrays]


def params(megabytes):
    return pltpu.CompilerParams(vmem_limit_bytes=megabytes << 20)


def cost(flops, moved):
    return pl.CostEstimate(flops=flops, bytes_accessed=moved, transcendentals=0)


def split_kernel(where, amp, keep, give):
    for k, out in enumerate((keep, give)):
        for a in range(4):
            row = pl.multiple_of(where[2 * a + k] * 64, 64)
            out[a * 64 : a * 64 + 64, :] = amp[pl.ds(row, 64), :].astype(BF)


def split(amp, where):
    return pl.pallas_call(
        split_kernel,
        out_shape=[jax.ShapeDtypeStruct((256, 1024), BF)] * 2,
        in_specs=[SMEM, VMEM],
        out_specs=[VMEM] * 2,
        compiler_params=params(8),
        cost_estimate=cost(0, 3 << 20),
        name="split",
    )(where, amp)


def weave_kernel(where, keep, got, *outs):
    own = pl.multiple_of(where[0] * 1024, 1024)
    oth = pl.multiple_of(1024 - where[0] * 1024, 1024)
    for a, out in enumerate(outs):
        out[:, pl.ds(own, 1024)] = keep[a * 64 : a * 64 + 64, :]
        out[:, pl.ds(oth, 1024)] = got[a * 64 : a * 64 + 64, :]


def weave(where, keep, got):
    return pl.pallas_call(
        weave_kernel,
        out_shape=[jax.ShapeDtypeStruct((64, 2048), BF)] * 4,
        in_specs=[SMEM] + [VMEM] * 2,
        out_specs=[VMEM] * 4,
        compiler_params=params(6),
        cost_estimate=cost(0, 2 << 20),
        name="weave",
    )(where, keep, got)


def join_kernel(where, *refs):
    out = refs[-1]
    for k in range(2):
        out[pl.ds(pl.multiple_of(where[k] * 64, 64), 64), :] = refs[k][...]


def join(where, pieces):
    return pl.pallas_call(
        join_kernel,
        out_shape=jax.ShapeDtypeStruct((128, 2048), BF),
        in_specs=[SMEM] + [VMEM] * 2,
        out_specs=VMEM,
        compiler_params=params(3),
        cost_estimate=cost(0, 1 << 20),
        name="join",
    )(where, *pieces)


def product_kernel(steps, odd, *refs):
    n = len(steps)
    n_in = 2 * n
    blocks = refs[:n_in]
    own, oth = refs[n_in : n_in + 2]
    zero_a, zero_b, one_a, three_b, up, down = refs[n_in + 2 : n_in + 8]
    held, keep_a, keep_b, panel, sems = refs[n_in + 8 :]

    def load(source, k, j):
        cols = pl.ds(pl.multiple_of(j * 512, 512), 512)
        return pltpu.make_async_copy(source.at[:, cols], panel.at[2 * k + j], sems.at[2 * k + j])

    for k in range(2):
        for j in range(2):
            load((own, oth)[k], k, j).start()
    for i in range(n):
        for h in range(2):
            offset = lax.bitwise_and(odd[0] + steps[i] + h, 1)
            for k in range(2):
                at = pl.multiple_of(i * 256 + k * 128 + offset * 64, 64)
                held[pl.ds(at, 64), :] = blocks[2 * i + h][k * 64 : k * 64 + 64, :]

    def rows_of(r, i, k):
        return r[i * 256 + k * 64 : i * 256 + k * 64 + 64]

    def first(j, carry):
        cols = pl.ds(pl.multiple_of(j * 512, 512), 512)
        load(own, 0, j).wait()
        r = jnp.dot(held[...], panel[j], preferred_element_type=F32)
        for i in range(n):
            at = slice(i * 64, i * 64 + 64)
            keep_a[at, cols] = rows_of(r, i, 0)
            one_a[at, cols] = rows_of(r, i, 1)
            up[at, cols] = rows_of(r, i, 2).astype(BF)
            down[at, cols] = rows_of(r, i, 3).astype(BF)
        return carry

    def second(j, carry):
        cols = pl.ds(pl.multiple_of(j * 512, 512), 512)
        wide = pl.ds(pl.multiple_of(j * 512 + 1024, 512), 512)
        load(oth, 1, j).wait()
        r = jnp.dot(held[...], panel[2 + j], preferred_element_type=F32)
        for i in range(n):
            at = slice(i * 64, i * 64 + 64)
            keep_b[at, cols] = rows_of(r, i, 0)
            up[at, wide] = rows_of(r, i, 1).astype(BF)
            down[at, wide] = rows_of(r, i, 2).astype(BF)
            three_b[at, cols] = rows_of(r, i, 3)
        return carry

    lax.fori_loop(0, 2, first, 0)
    copy_a = pltpu.make_async_copy(keep_a, zero_a, sems.at[4])
    copy_a.start()
    lax.fori_loop(0, 2, second, 0)
    copy_b = pltpu.make_async_copy(keep_b, zero_b, sems.at[5])
    copy_b.start()
    copy_a.wait()
    copy_b.wait()


def product(odd, steps, halves, own, oth):
    n = len(steps)
    half = jax.ShapeDtypeStruct((n * 64, 1024), F32)
    full = jax.ShapeDtypeStruct((n * 64, 2048), BF)
    return pl.pallas_call(
        functools.partial(product_kernel, steps),
        out_shape=[pltpu.HBM(half.shape, F32)] * 2 + [half] * 2 + [full] * 2,
        in_specs=[SMEM] + [VMEM] * (2 * n) + [ANY] * 2,
        out_specs=[HBM] * 2 + [VMEM] * 4,
        scratch_shapes=[
            pltpu.VMEM((n * 256, 2048), BF),
            pltpu.VMEM((n * 64, 1024), F32),
            pltpu.VMEM((n * 64, 1024), F32),
            pltpu.VMEM((4, 2048, 512), BF),
            pltpu.SemaphoreType.DMA((6,)),
        ],
        compiler_params=params(28),
        cost_estimate=cost(2 * n * 256 * 2048 * 2048, (9 << 20) + n * (3 << 20)),
        name="product",
    )(odd, *halves, *off_chip(own, oth))


def collect_kernel(n_groups, members, low, *refs):
    ins = refs[: 6 * n_groups]
    stay_a, stay_b, leave_a, leave_b = refs[6 * n_groups : 6 * n_groups + 4]
    wide, thin, sems = refs[6 * n_groups + 4 :]
    chunks = [q for pair in members for q in pair]
    copies = []
    for k, (g, n) in enumerate(chunks):
        za, zb, up, down, nup, ndown = ins[6 * g : 6 * g + 6]
        at = pl.ds(n * 64, 64)
        pairs = (
            (za.at[at, :], wide.at[2 * k]),
            (zb.at[at, :], wide.at[2 * k + 1]),
            (down.at[at, pl.ds(0, 1024)], thin.at[4 * k]),
            (nup.at[at, :], thin.at[4 * k + 1]),
            (up.at[at, pl.ds(1024, 1024)], thin.at[4 * k + 2]),
            (ndown.at[at, :], thin.at[4 * k + 3]),
        )
        copies += [pltpu.make_async_copy(a, b, sems.at[6 * k + j]) for j, (a, b) in enumerate(pairs)]
    for copy in copies:
        copy.start()
    for copy in copies:
        copy.wait()

    def total(k):
        a = wide[2 * k] + thin[4 * k].astype(F32) + thin[4 * k + 1].astype(F32)
        b = wide[2 * k + 1] + thin[4 * k + 2].astype(F32) + thin[4 * k + 3].astype(F32)
        return a, b

    def write(swap):
        for k in range(len(members)):
            at = slice(k * 64, k * 64 + 64)
            a, b = total(2 * k + swap)
            stay_a[at, :] = a
            stay_b[at, :] = b
            a, b = total(2 * k + 1 - swap)
            leave_a[at, :] = a.astype(BF)
            leave_b[at, :] = b.astype(BF)

    @pl.when(low[0] == 1)
    def _():
        write(0)

    @pl.when(low[0] == 0)
    def _():
        write(1)


def collect(low, groups, members):
    rows = 64 * len(members)
    flat = []
    for g in groups:
        flat += off_chip(*g[:2]) + (off_chip(*g[2:]) if len(groups) > 1 else list(g[2:]))
    n = 2 * len(members)
    return pl.pallas_call(
        functools.partial(collect_kernel, len(groups), members),
        out_shape=[jax.ShapeDtypeStruct((rows, 1024), F32)] * 2
        + [jax.ShapeDtypeStruct((rows, 1024), BF)] * 2,
        in_specs=[SMEM] + [ANY] * len(flat),
        out_specs=[VMEM] * 4,
        scratch_shapes=[
            pltpu.VMEM((2 * n, 64, 1024), F32),
            pltpu.VMEM((4 * n, 64, 1024), BF),
            pltpu.SemaphoreType.DMA((6 * n,)),
        ],
        compiler_params=params(12),
        cost_estimate=cost(0, rows * 1024 * 24),
        name="collect",
    )(low, *flat)


def index_kernel(place, slots, mask, inverse, code, row_of, count):
    x = place[0]
    c = place[1]

    def clear(s, carry):
        count[s] = 0
        return carry

    lax.fori_loop(0, 128, clear, 0, unroll=8)

    def row(r, carry):
        i = lax.bitwise_and(lax.shift_right_logical(r, 4) - x + 4, 3)
        other = lax.bitwise_xor(lax.bitwise_and(lax.shift_right_logical(r, 3), 1), c)
        part = other * 4 + lax.bitwise_xor(i, lax.shift_right_logical(i, 1))
        at = part * 8 + lax.bitwise_and(r, 7)
        row_of[r] = at * 8
        for k in range(8):
            t = r * 8 + k
            s = slots[t]
            n = count[s]
            count[s] = n + 1
            q = s * 4 + n
            inverse[t] = q
            code[q] = at * 16 + k * 2 + mask[t]
        return carry

    lax.fori_loop(0, 64, row, 0)


def index(place, slots, mask):
    return pl.pallas_call(
        index_kernel,
        out_shape=[jax.ShapeDtypeStruct((n,), jnp.int32) for n in (512, 512, 64)],
        in_specs=[SMEM] * 3,
        out_specs=[SMEM] * 3,
        scratch_shapes=[pltpu.SMEM((128,), jnp.int32)],
        compiler_params=params(1),
        cost_estimate=cost(0, 8 << 10),
        name="index",
    )(place, slots, mask)


def outgoing_kernel(code, *refs):
    ins = refs[:12]
    full, out = refs[12:14]
    full_v, out_v, wide, thin, sems = refs[14:]
    copies = []
    at = 0
    for k in (0, 2):
        for g in range(2):
            stay, got = ins[4 * g + k : 4 * g + k + 2]
            rows = stay.shape[0]
            n = len(copies)
            copies += [
                pltpu.make_async_copy(stay, wide.at[pl.ds(at, rows), :], sems.at[n]),
                pltpu.make_async_copy(got, thin.at[pl.ds(at, rows), :], sems.at[n + 1]),
            ]
            at += rows
    for copy in copies:
        copy.start()
    for k, to in ((0, 192), (2, 448)):
        stay, got = ins[8 + k : 8 + k + 2]
        full_v[to : to + 64, :] = stay[...] + got[...].astype(F32)
    for copy in copies:
        copy.wait()
    for at, to in ((0, 0), (192, 256)):
        full_v[to : to + 192, :] = wide[at : at + 192, :] + thin[at : at + 192, :].astype(F32)
    save = pltpu.make_async_copy(full_v, full, sems.at[8])
    save.start()

    def gather(s, carry):
        rows = []
        for j in range(4):
            q = code[s * 4 + j]
            row = pl.multiple_of(lax.shift_right_logical(q, 4) * 8, 8)
            col = pl.multiple_of(lax.bitwise_and(lax.shift_right_logical(q, 1), 7) * 128, 128)
            w = lax.bitwise_and(q, 1).astype(F32)
            rows.append(full_v[pl.ds(row, 8), pl.ds(col, 128)] * w)
        out_v[s] = jnp.concatenate(rows, axis=0).astype(BF)
        return carry

    sends = []
    for k in range(4):
        part = pl.ds(32 * k, 32)
        lax.fori_loop(32 * k, 32 * k + 32, gather, 0, unroll=4)
        sends.append(pltpu.make_async_copy(out_v.at[part], out.at[part], sems.at[9 + k]))
        sends[-1].start()
    for copy in sends:
        copy.wait()
    save.wait()


def outgoing(code, *parts):
    return pl.pallas_call(
        outgoing_kernel,
        out_shape=[pltpu.HBM((512, 1024), F32), pltpu.HBM((128, 32, 128), BF)],
        in_specs=[SMEM] + [ANY] * 8 + [VMEM] * 4,
        out_specs=[HBM] * 2,
        scratch_shapes=[
            pltpu.VMEM((512, 1024), F32),
            pltpu.VMEM((128, 32, 128), BF),
            pltpu.VMEM((384, 1024), F32),
            pltpu.VMEM((384, 1024), BF),
            pltpu.SemaphoreType.DMA((13,)),
        ],
        compiler_params=params(12),
        cost_estimate=cost(0, 6 << 20),
        name="outgoing",
    )(code, *parts)


def base_kernel(row_of, mask, full, amp, occ, vir, base, scale):
    def row(r, carry):
        at = pl.multiple_of(r * 8, 8)
        src = pl.multiple_of(row_of[r], 8)
        e = occ[pl.ds(at, 8), :]
        for k in range(8):
            w = mask[r * 8 + k].astype(F32)
            cols = slice(k * 128, k * 128 + 128)
            q = 1.0 / (e + vir[:, cols])
            scale[pl.ds(at, 8), cols] = q
            base[pl.ds(at, 8), cols] = amp[pl.ds(at, 8), cols] - full[pl.ds(src, 8), cols] * w * q
        return carry

    lax.fori_loop(0, 64, row, 0, unroll=2)


def make_base(row_of, mask, full, amp, occ, vir):
    return pl.pallas_call(
        base_kernel,
        out_shape=[jax.ShapeDtypeStruct((512, 1024), F32)] * 2,
        in_specs=[SMEM] * 2 + [VMEM] * 4,
        out_specs=[VMEM] * 2,
        compiler_params=params(14),
        cost_estimate=cost(0, 8 << 20),
        name="base",
    )(row_of, mask, full, amp, occ, vir)


def update_kernel(inverse, incoming, base, scale, out, wide, base_v, scale_v, out_v, sems):
    loads = []
    for k in range(4):
        part = pl.ds(128 * k, 128)
        loads.append(
            (
                pltpu.make_async_copy(base.at[part, :], base_v.at[part, :], sems.at[3 * k]),
                pltpu.make_async_copy(scale.at[part, :], scale_v.at[part, :], sems.at[3 * k + 1]),
            )
        )
    for pair in loads:
        for copy in pair:
            copy.start()
    wide[...] = incoming[...].astype(F32)

    def row(r, carry):
        at = pl.multiple_of(r * 8, 8)
        for k in range(8):
            q = inverse[r * 8 + k]
            partner = wide[pl.ds(pl.multiple_of(q * 8, 8), 8), :]
            cols = slice(k * 128, k * 128 + 128)
            out_v[pl.ds(at, 8), cols] = (
                base_v[pl.ds(at, 8), cols] - partner * scale_v[pl.ds(at, 8), cols]
            )
        return carry

    stores = []
    for k in range(4):
        for copy in loads[k]:
            copy.wait()
        lax.fori_loop(16 * k, 16 * k + 16, row, 0, unroll=4)
        part = pl.ds(128 * k, 128)
        stores.append(pltpu.make_async_copy(out_v.at[part, :], out.at[part, :], sems.at[3 * k + 2]))
        stores[-1].start()
    for copy in stores:
        copy.wait()


def update(inverse, incoming, base, scale):
    return pl.pallas_call(
        update_kernel,
        out_shape=jax.ShapeDtypeStruct((512, 1024), F32),
        in_specs=[SMEM, VMEM, HBM, HBM],
        out_specs=HBM,
        scratch_shapes=[
            pltpu.VMEM((4096, 128), F32),
            pltpu.VMEM((512, 1024), F32),
            pltpu.VMEM((512, 1024), F32),
            pltpu.VMEM((512, 1024), F32),
            pltpu.SemaphoreType.DMA((12,)),
        ],
        compiler_params=params(14),
        cost_estimate=cost(0, 7 << 20),
        name="update",
    )(inverse, incoming, *off_chip(base, scale))


GROUPS = (((0, 0),), ((0, 1), (1, 0), (3, 0)), ((1, 1), (3, 1)), ((2, 0), (2, 1)))
LAST = (
    ((0, 1), (((0, 0), (1, 0)),)),
    ((1, 2), (((0, 1), (1, 0)), ((0, 2), (1, 1)))),
    ((3,), (((0, 0), (0, 1)),)),
)


def compute(amplitudes, integrals, occ_energy, vir_energy, tile_mask, partner_slot):
    device = lax.axis_index(AXES)
    c, x, zh = device & 1, (device >> 1) & 3, (device >> 3) & 1
    y = (device >> 5) & 3
    fy = 2 * zh + (x >> 1)

    where = jnp.stack([((y - fy + a) & 3) * 2 + (c ^ b) for a in range(4) for b in range(2)])
    keep, give = split(amplitudes, where)
    got = send(give, shift(dc=1))
    pieces = weave(c[None], keep, got)
    moved = [send(pieces[a], spread(a)) for a in range(4)]
    own = integrals
    oth = send(integrals, shift(dc=1))
    half = {}
    for h in range(2):
        where = jnp.stack([((x - a) & 3) >> 1 for a in (h, h + 2)])
        half[0, 0, h] = join(where, [moved[h], moved[h + 2]])

    for h in range(2):
        half[1, 0, h] = send(half[0, 0, h], shift(dx=-1))
        half[3, 0, h] = send(half[0, 0, h], shift(dx=1))
        half[0, 1, h] = send(half[0, 0, h], shift(dzh=1))
        half[1, 1, h] = send(half[0, 1, h], shift(dx=-1))
        half[3, 1, h] = send(half[0, 1, h], shift(dx=1))
    for j in range(2):
        half[2, j, 0] = send(half[1, j, 0], shift(dx=-1))
        half[2, j, 1] = send(half[3, j, 1], shift(dx=1))

    odd = (x & 1)[None]
    sums = []
    for group in GROUPS:
        halves = [half[i, j, h] for i, j in group for h in range(2)]
        za, zb, one_a, three_b, up, down = product(
            odd, tuple(i for i, j in group), halves, own, oth
        )
        up = send(up, shift(dy=1))
        down = send(down, shift(dy=-1))
        nup = (one_a + up[:, :1024].astype(F32)).astype(BF)
        ndown = (three_b + down[:, 1024:].astype(F32)).astype(BF)
        nup = send(nup, shift(dy=1))
        ndown = send(ndown, shift(dy=-1))
        sums.append((za, zb, up, down, nup, ndown))

    low = (zh == ((device >> 4) & 1)).astype(jnp.int32)[None]
    last = []
    for groups, members in LAST:
        stay_a, stay_b, leave_a, leave_b = collect(low, [sums[k] for k in groups], members)
        got_a = send(leave_a, shift(dzl=1))
        got_b = send(leave_b, shift(dzl=1, dc=1))
        stay_b = send(stay_b, shift(dc=1))
        last += [stay_a, got_a, stay_b, got_b]

    mask = tile_mask.reshape(-1)
    inverse, code, row_of = index(jnp.stack([x, c]), partner_slot.reshape(-1), mask)
    full, out = outgoing(code, *last)
    incoming = lax.all_to_all(out, AXES, split_axis=0, concat_axis=0, tiled=True)
    base, scale = make_base(
        row_of, mask, full, amplitudes, occ_energy[:, None], vir_energy[None, :]
    )
    return update(inverse, incoming.reshape(4096, 128), base, scale)


def solution(mesh):
    in_specs = (
        P("pair", "virt"),
        P("pair", "virt"),
        P("pair"),
        P("virt"),
        P("pair", "virt"),
        P("pair", "virt"),
    )
    out_specs = P("pair", "virt")
    return jax.shard_map(compute, mesh=mesh, in_specs=in_specs, out_specs=out_specs, check_vma=False)
```

```python
import functools
import jax
import jax.numpy as jnp
from jax import lax
from jax.experimental import pallas as pl
from jax.experimental.pallas import tpu as pltpu
from jax.sharding import PartitionSpec as P

AXES = ("pair", "virt")
BF = jnp.bfloat16
F32 = jnp.float32


def decode(device):
    p, v = divmod(device, 16)
    y, zl = divmod(p, 2)
    zh, r = divmod(v, 8)
    x, c = divmod(r, 2)
    return x, y, zl, zh, c


def encode(x, y, zl, zh, c):
    return ((y % 4) * 2 + zl % 2) * 16 + (zh % 2) * 8 + (x % 4) * 2 + c % 2


def permutation(move):
    return [(d, encode(*move(*decode(d)))) for d in range(128)]


def shift(dx=0, dy=0, dzl=0, dzh=0, dc=0):
    return permutation(lambda x, y, zl, zh, c: (x + dx, y + dy, zl + dzl, zh + dzh, c + dc))


def spread(a):
    def move(x, y, zl, zh, c):
        fy, fzl = 2 * zh + x // 2, x % 2
        return (y - fy + a, fy, fzl, zl, c)

    return permutation(move)


def send(value, pairs):
    return lax.ppermute(value, AXES, pairs)


VMEM = pl.BlockSpec(memory_space=pltpu.VMEM)
SMEM = pl.BlockSpec(memory_space=pltpu.SMEM)
HBM = pl.BlockSpec(memory_space=pltpu.HBM)
ANY = pl.BlockSpec(memory_space=pl.ANY)


def off_chip(*arrays):
    return [pltpu.with_memory_space_constraint(a, pltpu.HBM) for a in arrays]


def params(megabytes):
    return pltpu.CompilerParams(vmem_limit_bytes=megabytes << 20)


def cost(flops, moved):
    return pl.CostEstimate(flops=flops, bytes_accessed=moved, transcendentals=0)


def split_kernel(where, amp, keep, give):
    for k, out in enumerate((keep, give)):
        for a in range(4):
            row = pl.multiple_of(where[2 * a + k] * 64, 64)
            out[a * 64 : a * 64 + 64, :] = amp[pl.ds(row, 64), :].astype(BF)


def split(amp, where):
    return pl.pallas_call(
        split_kernel,
        out_shape=[jax.ShapeDtypeStruct((256, 1024), BF)] * 2,
        in_specs=[SMEM, VMEM],
        out_specs=[VMEM] * 2,
        compiler_params=params(8),
        cost_estimate=cost(0, 3 << 20),
        name="split",
    )(where, amp)


def weave_kernel(where, keep, got, *outs):
    own = pl.multiple_of(where[0] * 1024, 1024)
    oth = pl.multiple_of(1024 - where[0] * 1024, 1024)
    for a, out in enumerate(outs):
        out[:, pl.ds(own, 1024)] = keep[a * 64 : a * 64 + 64, :]
        out[:, pl.ds(oth, 1024)] = got[a * 64 : a * 64 + 64, :]


def weave(where, keep, got):
    return pl.pallas_call(
        weave_kernel,
        out_shape=[jax.ShapeDtypeStruct((64, 2048), BF)] * 4,
        in_specs=[SMEM] + [VMEM] * 2,
        out_specs=[VMEM] * 4,
        compiler_params=params(6),
        cost_estimate=cost(0, 2 << 20),
        name="weave",
    )(where, keep, got)


def join_kernel(where, *refs):
    out = refs[-1]
    for k in range(2):
        out[pl.ds(pl.multiple_of(where[k] * 64, 64), 64), :] = refs[k][...]


def join(where, pieces):
    return pl.pallas_call(
        join_kernel,
        out_shape=jax.ShapeDtypeStruct((128, 2048), BF),
        in_specs=[SMEM] + [VMEM] * 2,
        out_specs=VMEM,
        compiler_params=params(3),
        cost_estimate=cost(0, 1 << 20),
        name="join",
    )(where, *pieces)


def product_kernel(steps, odd, *refs):
    n = len(steps)
    n_in = 2 * n
    blocks = refs[:n_in]
    own, oth = refs[n_in : n_in + 2]
    zero_a, zero_b, one_a, three_b, up, down = refs[n_in + 2 : n_in + 8]
    held, keep_a, keep_b, panel, sems = refs[n_in + 8 :]

    def load(source, k, j):
        cols = pl.ds(pl.multiple_of(j * 512, 512), 512)
        return pltpu.make_async_copy(source.at[:, cols], panel.at[2 * k + j], sems.at[2 * k + j])

    for k in range(2):
        for j in range(2):
            load((own, oth)[k], k, j).start()
    for i in range(n):
        for h in range(2):
            offset = lax.bitwise_and(odd[0] + steps[i] + h, 1)
            for k in range(2):
                at = pl.multiple_of(i * 256 + k * 128 + offset * 64, 64)
                held[pl.ds(at, 64), :] = blocks[2 * i + h][k * 64 : k * 64 + 64, :]

    def rows_of(r, i, k):
        return r[i * 256 + k * 64 : i * 256 + k * 64 + 64]

    def first(j, carry):
        cols = pl.ds(pl.multiple_of(j * 512, 512), 512)
        load(own, 0, j).wait()
        r = jnp.dot(held[...], panel[j], preferred_element_type=F32)
        for i in range(n):
            at = slice(i * 64, i * 64 + 64)
            keep_a[at, cols] = rows_of(r, i, 0)
            one_a[at, cols] = rows_of(r, i, 1)
            up[at, cols] = rows_of(r, i, 2).astype(BF)
            down[at, cols] = rows_of(r, i, 3).astype(BF)
        return carry

    def second(j, carry):
        cols = pl.ds(pl.multiple_of(j * 512, 512), 512)
        wide = pl.ds(pl.multiple_of(j * 512 + 1024, 512), 512)
        load(oth, 1, j).wait()
        r = jnp.dot(held[...], panel[2 + j], preferred_element_type=F32)
        for i in range(n):
            at = slice(i * 64, i * 64 + 64)
            keep_b[at, cols] = rows_of(r, i, 0)
            up[at, wide] = rows_of(r, i, 1).astype(BF)
            down[at, wide] = rows_of(r, i, 2).astype(BF)
            three_b[at, cols] = rows_of(r, i, 3)
        return carry

    lax.fori_loop(0, 2, first, 0)
    copy_a = pltpu.make_async_copy(keep_a, zero_a, sems.at[4])
    copy_a.start()
    lax.fori_loop(0, 2, second, 0)
    copy_b = pltpu.make_async_copy(keep_b, zero_b, sems.at[5])
    copy_b.start()
    copy_a.wait()
    copy_b.wait()


def product(odd, steps, halves, own, oth):
    n = len(steps)
    half = jax.ShapeDtypeStruct((n * 64, 1024), F32)
    full = jax.ShapeDtypeStruct((n * 64, 2048), BF)
    return pl.pallas_call(
        functools.partial(product_kernel, steps),
        out_shape=[pltpu.HBM(half.shape, F32)] * 2 + [half] * 2 + [full] * 2,
        in_specs=[SMEM] + [VMEM] * (2 * n) + [ANY] * 2,
        out_specs=[HBM] * 2 + [VMEM] * 4,
        scratch_shapes=[
            pltpu.VMEM((n * 256, 2048), BF),
            pltpu.VMEM((n * 64, 1024), F32),
            pltpu.VMEM((n * 64, 1024), F32),
            pltpu.VMEM((4, 2048, 512), BF),
            pltpu.SemaphoreType.DMA((6,)),
        ],
        compiler_params=params(28),
        cost_estimate=cost(2 * n * 256 * 2048 * 2048, (9 << 20) + n * (3 << 20)),
        name="product",
    )(odd, *halves, *off_chip(own, oth))


def collect_kernel(n_groups, members, low, *refs):
    ins = refs[: 6 * n_groups]
    stay_a, stay_b, leave_a, leave_b = refs[6 * n_groups : 6 * n_groups + 4]
    wide, thin, sems = refs[6 * n_groups + 4 :]
    chunks = [q for pair in members for q in pair]
    copies = []
    for k, (g, n) in enumerate(chunks):
        za, zb, up, down, nup, ndown = ins[6 * g : 6 * g + 6]
        at = pl.ds(n * 64, 64)
        pairs = (
            (za.at[at, :], wide.at[2 * k]),
            (zb.at[at, :], wide.at[2 * k + 1]),
            (down.at[at, pl.ds(0, 1024)], thin.at[4 * k]),
            (nup.at[at, :], thin.at[4 * k + 1]),
            (up.at[at, pl.ds(1024, 1024)], thin.at[4 * k + 2]),
            (ndown.at[at, :], thin.at[4 * k + 3]),
        )
        copies += [pltpu.make_async_copy(a, b, sems.at[6 * k + j]) for j, (a, b) in enumerate(pairs)]
    for copy in copies:
        copy.start()
    for copy in copies:
        copy.wait()

    def total(k):
        a = wide[2 * k] + thin[4 * k].astype(F32) + thin[4 * k + 1].astype(F32)
        b = wide[2 * k + 1] + thin[4 * k + 2].astype(F32) + thin[4 * k + 3].astype(F32)
        return a, b

    def write(swap):
        for k in range(len(members)):
            at = slice(k * 64, k * 64 + 64)
            a, b = total(2 * k + swap)
            stay_a[at, :] = a
            stay_b[at, :] = b
            a, b = total(2 * k + 1 - swap)
            leave_a[at, :] = a.astype(BF)
            leave_b[at, :] = b.astype(BF)

    @pl.when(low[0] == 1)
    def _():
        write(0)

    @pl.when(low[0] == 0)
    def _():
        write(1)


def collect(low, groups, members):
    rows = 64 * len(members)
    flat = []
    for g in groups:
        flat += off_chip(*g[:2]) + (off_chip(*g[2:]) if len(groups) > 1 else list(g[2:]))
    n = 2 * len(members)
    return pl.pallas_call(
        functools.partial(collect_kernel, len(groups), members),
        out_shape=[jax.ShapeDtypeStruct((rows, 1024), F32)] * 2
        + [jax.ShapeDtypeStruct((rows, 1024), BF)] * 2,
        in_specs=[SMEM] + [ANY] * len(flat),
        out_specs=[VMEM] * 4,
        scratch_shapes=[
            pltpu.VMEM((2 * n, 64, 1024), F32),
            pltpu.VMEM((4 * n, 64, 1024), BF),
            pltpu.SemaphoreType.DMA((6 * n,)),
        ],
        compiler_params=params(12),
        cost_estimate=cost(0, rows * 1024 * 24),
        name="collect",
    )(low, *flat)


def index_kernel(place, slots, mask, inverse, code, row_of, count):
    x = place[0]
    c = place[1]

    def clear(s, carry):
        count[s] = 0
        return carry

    lax.fori_loop(0, 128, clear, 0, unroll=8)

    def row(r, carry):
        i = lax.bitwise_and(lax.shift_right_logical(r, 4) - x + 4, 3)
        other = lax.bitwise_xor(lax.bitwise_and(lax.shift_right_logical(r, 3), 1), c)
        part = other * 4 + lax.bitwise_xor(i, lax.shift_right_logical(i, 1))
        at = part * 8 + lax.bitwise_and(r, 7)
        row_of[r] = at * 8
        for k in range(8):
            t = r * 8 + k
            s = slots[t]
            n = count[s]
            count[s] = n + 1
            q = s * 4 + n
            inverse[t] = q
            code[q] = at * 16 + k * 2 + mask[t]
        return carry

    lax.fori_loop(0, 64, row, 0)


def index(place, slots, mask):
    return pl.pallas_call(
        index_kernel,
        out_shape=[jax.ShapeDtypeStruct((n,), jnp.int32) for n in (512, 512, 64)],
        in_specs=[SMEM] * 3,
        out_specs=[SMEM] * 3,
        scratch_shapes=[pltpu.SMEM((128,), jnp.int32)],
        compiler_params=params(1),
        cost_estimate=cost(0, 8 << 10),
        name="index",
    )(place, slots, mask)


def prefill_kernel(*refs):
    ins, out, wide, thin, sems = refs[:8], refs[8], refs[9], refs[10], refs[11]
    copies = []
    at = 0
    for k in (0, 2):
        for g in range(2):
            stay, got = ins[4 * g + k : 4 * g + k + 2]
            rows = stay.shape[0]
            n = len(copies)
            copies += [
                pltpu.make_async_copy(stay, wide.at[pl.ds(at, rows), :], sems.at[n]),
                pltpu.make_async_copy(got, thin.at[pl.ds(at, rows), :], sems.at[n + 1]),
            ]
            at += rows
    for copy in copies:
        copy.start()
    for copy in copies:
        copy.wait()
    out[...] = wide[...] + thin[...].astype(F32)


def prefill(*parts):
    return pl.pallas_call(
        prefill_kernel,
        out_shape=jax.ShapeDtypeStruct((384, 1024), F32),
        in_specs=[ANY] * 8,
        out_specs=VMEM,
        scratch_shapes=[
            pltpu.VMEM((384, 1024), F32),
            pltpu.VMEM((384, 1024), BF),
            pltpu.SemaphoreType.DMA((8,)),
        ],
        compiler_params=params(8),
        cost_estimate=cost(0, 4 << 20),
        name="prefill",
    )(*parts)


def outgoing_kernel(code, ready, *refs):
    ins = refs[:4]
    full, out = refs[4:6]
    full_v, out_v, sems = refs[6:]
    for k, at, to in ((0, 0, 0), (2, 192, 256)):
        full_v[to : to + 192, :] = ready[at : at + 192, :]
        stay, got = ins[k : k + 2]
        full_v[to + 192 : to + 256, :] = stay[...] + got[...].astype(F32)
    save = pltpu.make_async_copy(full_v, full, sems.at[0])
    save.start()

    def gather(s, carry):
        rows = []
        for j in range(4):
            q = code[s * 4 + j]
            row = pl.multiple_of(lax.shift_right_logical(q, 4) * 8, 8)
            col = pl.multiple_of(lax.bitwise_and(lax.shift_right_logical(q, 1), 7) * 128, 128)
            w = lax.bitwise_and(q, 1).astype(F32)
            rows.append(full_v[pl.ds(row, 8), pl.ds(col, 128)] * w)
        out_v[s] = jnp.concatenate(rows, axis=0).astype(BF)
        return carry

    sends = []
    for k in range(4):
        part = pl.ds(32 * k, 32)
        lax.fori_loop(32 * k, 32 * k + 32, gather, 0, unroll=4)
        sends.append(pltpu.make_async_copy(out_v.at[part], out.at[part], sems.at[1 + k]))
        sends[-1].start()
    for copy in sends:
        copy.wait()
    save.wait()


def outgoing(code, ready, *parts):
    return pl.pallas_call(
        outgoing_kernel,
        out_shape=[pltpu.HBM((512, 1024), F32), pltpu.HBM((128, 32, 128), BF)],
        in_specs=[SMEM] + [VMEM] * 5,
        out_specs=[HBM] * 2,
        scratch_shapes=[
            pltpu.VMEM((512, 1024), F32),
            pltpu.VMEM((128, 32, 128), BF),
            pltpu.SemaphoreType.DMA((5,)),
        ],
        compiler_params=params(12),
        cost_estimate=cost(0, 6 << 20),
        name="outgoing",
    )(code, ready, *parts)


def base_kernel(row_of, mask, full, amp, occ, vir, base, scale):
    def row(r, carry):
        at = pl.multiple_of(r * 8, 8)
        src = pl.multiple_of(row_of[r], 8)
        e = occ[pl.ds(at, 8), :]
        for k in range(8):
            w = mask[r * 8 + k].astype(F32)
            cols = slice(k * 128, k * 128 + 128)
            q = 1.0 / (e + vir[:, cols])
            scale[pl.ds(at, 8), cols] = q
            base[pl.ds(at, 8), cols] = amp[pl.ds(at, 8), cols] - full[pl.ds(src, 8), cols] * w * q
        return carry

    lax.fori_loop(0, 64, row, 0, unroll=2)


def make_base(row_of, mask, full, amp, occ, vir):
    return pl.pallas_call(
        base_kernel,
        out_shape=[jax.ShapeDtypeStruct((512, 1024), F32)] * 2,
        in_specs=[SMEM] * 2 + [VMEM] * 4,
        out_specs=[VMEM] * 2,
        compiler_params=params(14),
        cost_estimate=cost(0, 8 << 20),
        name="base",
    )(row_of, mask, full, amp, occ, vir)


def update_kernel(inverse, incoming, base, scale, out, wide, base_v, scale_v, out_v, sems):
    loads = []
    for k in range(4):
        part = pl.ds(128 * k, 128)
        loads.append(
            (
                pltpu.make_async_copy(base.at[part, :], base_v.at[part, :], sems.at[3 * k]),
                pltpu.make_async_copy(scale.at[part, :], scale_v.at[part, :], sems.at[3 * k + 1]),
            )
        )
    for pair in loads:
        for copy in pair:
            copy.start()
    wide[...] = incoming[...].astype(F32)

    def row(r, carry):
        at = pl.multiple_of(r * 8, 8)
        for k in range(8):
            q = inverse[r * 8 + k]
            partner = wide[pl.ds(pl.multiple_of(q * 8, 8), 8), :]
            cols = slice(k * 128, k * 128 + 128)
            out_v[pl.ds(at, 8), cols] = (
                base_v[pl.ds(at, 8), cols] - partner * scale_v[pl.ds(at, 8), cols]
            )
        return carry

    stores = []
    for k in range(4):
        for copy in loads[k]:
            copy.wait()
        lax.fori_loop(16 * k, 16 * k + 16, row, 0, unroll=4)
        part = pl.ds(128 * k, 128)
        stores.append(pltpu.make_async_copy(out_v.at[part, :], out.at[part, :], sems.at[3 * k + 2]))
        stores[-1].start()
    for copy in stores:
        copy.wait()


def update(inverse, incoming, base, scale):
    return pl.pallas_call(
        update_kernel,
        out_shape=jax.ShapeDtypeStruct((512, 1024), F32),
        in_specs=[SMEM, VMEM, HBM, HBM],
        out_specs=HBM,
        scratch_shapes=[
            pltpu.VMEM((4096, 128), F32),
            pltpu.VMEM((512, 1024), F32),
            pltpu.VMEM((512, 1024), F32),
            pltpu.VMEM((512, 1024), F32),
            pltpu.SemaphoreType.DMA((12,)),
        ],
        compiler_params=params(14),
        cost_estimate=cost(0, 7 << 20),
        name="update",
    )(inverse, incoming, *off_chip(base, scale))


GROUPS = (((0, 0),), ((0, 1), (1, 0), (3, 0)), ((1, 1), (3, 1)), ((2, 0), (2, 1)))
LAST = (
    ((0, 1), (((0, 0), (1, 0)),)),
    ((1, 2), (((0, 1), (1, 0)), ((0, 2), (1, 1)))),
    ((3,), (((0, 0), (0, 1)),)),
)


def compute(amplitudes, integrals, occ_energy, vir_energy, tile_mask, partner_slot):
    device = lax.axis_index(AXES)
    c, x, zh = device & 1, (device >> 1) & 3, (device >> 3) & 1
    y = (device >> 5) & 3
    fy = 2 * zh + (x >> 1)

    where = jnp.stack([((y - fy + a) & 3) * 2 + (c ^ b) for a in range(4) for b in range(2)])
    keep, give = split(amplitudes, where)
    got = send(give, shift(dc=1))
    pieces = weave(c[None], keep, got)
    moved = [send(pieces[a], spread(a)) for a in range(4)]
    own = integrals
    oth = send(integrals, shift(dc=1))
    half = {}
    for h in range(2):
        where = jnp.stack([((x - a) & 3) >> 1 for a in (h, h + 2)])
        half[0, 0, h] = join(where, [moved[h], moved[h + 2]])

    for h in range(2):
        half[1, 0, h] = send(half[0, 0, h], shift(dx=-1))
        half[3, 0, h] = send(half[0, 0, h], shift(dx=1))
        half[0, 1, h] = send(half[0, 0, h], shift(dzh=1))
        half[1, 1, h] = send(half[0, 1, h], shift(dx=-1))
        half[3, 1, h] = send(half[0, 1, h], shift(dx=1))
    for j in range(2):
        half[2, j, 0] = send(half[1, j, 0], shift(dx=-1))
        half[2, j, 1] = send(half[3, j, 1], shift(dx=1))

    odd = (x & 1)[None]
    sums = []
    for group in GROUPS:
        halves = [half[i, j, h] for i, j in group for h in range(2)]
        za, zb, one_a, three_b, up, down = product(
            odd, tuple(i for i, j in group), halves, own, oth
        )
        up = send(up, shift(dy=1))
        down = send(down, shift(dy=-1))
        nup = (one_a + up[:, :1024].astype(F32)).astype(BF)
        ndown = (three_b + down[:, 1024:].astype(F32)).astype(BF)
        nup = send(nup, shift(dy=1))
        ndown = send(ndown, shift(dy=-1))
        sums.append((za, zb, up, down, nup, ndown))

    low = (zh == ((device >> 4) & 1)).astype(jnp.int32)[None]
    last = []
    for groups, members in LAST:
        stay_a, stay_b, leave_a, leave_b = collect(low, [sums[k] for k in groups], members)
        got_a = send(leave_a, shift(dzl=1))
        got_b = send(leave_b, shift(dzl=1, dc=1))
        stay_b = send(stay_b, shift(dc=1))
        last += [stay_a, got_a, stay_b, got_b]

    mask = tile_mask.reshape(-1)
    inverse, code, row_of = index(jnp.stack([x, c]), partner_slot.reshape(-1), mask)
    ready = prefill(*last[:8])
    full, out = outgoing(code, ready, *last[8:])
    incoming = lax.all_to_all(out, AXES, split_axis=0, concat_axis=0, tiled=True)
    base, scale = make_base(
        row_of, mask, full, amplitudes, occ_energy[:, None], vir_energy[None, :]
    )
    return update(inverse, incoming.reshape(4096, 128), base, scale)


def solution(mesh):
    in_specs = (
        P("pair", "virt"),
        P("pair", "virt"),
        P("pair"),
        P("virt"),
        P("pair", "virt"),
        P("pair", "virt"),
    )
    out_specs = P("pair", "virt")
    return jax.shard_map(compute, mesh=mesh, in_specs=in_specs, out_specs=out_specs, check_vma=False)
```
